256 devices in a mesh: row: 16 (over x_lo, y, core), col: 16 (over z, x_hi).
Axes of the slice: x: 4 (x_hi: 2, x_lo: 2; x = x_hi * 2 + x_lo), y: 4, z: 8, core: 2. Of those that a mesh axis runs over, the one named last changes fastest.
Arguments:
- a_panels: bfloat16 [16, 16, 16, 256, 256], P('row', 'col'), may hold values from -1.5 to 1.5
- b_panels: bfloat16 [16, 16, 16, 256, 256], P('row', 'col'), may hold values from -1.5 to 1.5
- a_rows: int32 [16, 16, 16], replicated, may hold values from 0 to 23, as said below
- a_inner: int32 [16, 16, 16], replicated, may hold values from 0 to 23, as said below
- b_inner: int32 [16, 16, 16], replicated, may hold values from 0 to 23, as said below
- b_cols: int32 [16, 16, 16], replicated, may hold values from 0 to 23, as said below
- c_rows: int32 [16, 16, 64], replicated, may hold values from 0 to 23, as said below
- c_cols: int32 [16, 16, 64], replicated, may hold values from 0 to 23
Outputs:
- c_blocks: bfloat16 [16, 16, 64, 256, 256], P('row', 'col')
The draws below stay inside these ranges and needn't reach their ends.
Inputs may be any that keep to these rules, and one draw needn't show every extreme that they name: `a_rows`: the blocks of one left panel stand at distinct positions; the left blocks and result blocks of one grid row use the same 8 block rows. `a_inner`: all left and right panels draw their inner indices from one common set of 8 indices, which holds 23; every left panel uses 24 - 1. `b_inner`: every right panel holds each index of the common set exactly twice. `b_cols`: the blocks of one right panel stand at distinct positions; the right blocks and result blocks of one grid column use the same 8 block columns. `c_rows`: the 64 result positions of one grid position are distinct and cover every pair of its grid row's block rows and its grid column's block columns.
All inputs are finite; a program needn't handle non-finite values.
Results may differ from the reference program's by a relative error of at most 0.001.
Values may be sent and summed in bfloat16 or wider, within the bound.
A program may use at most 128 MiB of HBM per device.

```python
import jax
import jax.numpy as jnp
from jax import lax

BS = 256
PB = 24
RACT = 8
NBLK = 16
NC = 64
STEPS = 4
ROWS_GRID = 16
COLS_GRID = 16


def pattern(key):
    key = jax.random.fold_in(key, 23)
    row_key, col_key, left_key, right_key, result_key, common_key = jax.random.split(key, 6)
    half_count = NBLK // 2

    def active(subkey):
        return jax.random.permutation(subkey, PB)[:RACT].astype(jnp.int32)
    act_rows = jax.vmap(active)(jax.random.split(row_key, ROWS_GRID))
    act_cols = jax.vmap(active)(jax.random.split(col_key, COLS_GRID))
    common_head = jax.random.permutation(common_key, PB - 1)[:half_count - 1].astype(jnp.int32)
    common_set = jnp.concatenate([common_head, jnp.full((1,), PB - 1, jnp.int32)])
    devices = jnp.arange(ROWS_GRID * COLS_GRID, dtype=jnp.int32)
    grid_rows = devices // COLS_GRID
    grid_cols = devices % COLS_GRID

    def left_one(subkey, grid_row):
        keys_two = jax.random.split(subkey, 2)
        forced_row = jax.random.randint(keys_two[0], (1,), 0, RACT, dtype=jnp.int32)
        forced = forced_row * half_count + (half_count - 1)
        others = jax.random.permutation(keys_two[1], RACT * half_count - 1)[:NBLK - 1].astype(jnp.int32)
        others = jnp.where(others >= forced[0], others + 1, others)
        chosen = jnp.concatenate([forced, others]).astype(jnp.int32)
        return (act_rows[grid_row][chosen // half_count], common_set[chosen % half_count])

    def right_one(subkey, grid_col):
        subkeys = jax.random.split(subkey, 3)
        order = jax.random.permutation(subkeys[0], half_count).astype(jnp.int32)
        first_col = jax.random.randint(subkeys[1], (half_count,), 0, RACT, dtype=jnp.int32)
        offsets = jax.random.randint(subkeys[2], (half_count,), 1, RACT, dtype=jnp.int32)
        second_col = (first_col + offsets) % RACT
        inner_index = jnp.concatenate([common_set, common_set[order]])
        column_index = jnp.concatenate([first_col, second_col[order]])
        return (inner_index, act_cols[grid_col][column_index])

    def result_one(subkey, grid_row, grid_col):
        chosen = jax.random.permutation(subkey, RACT * RACT)[:NC].astype(jnp.int32)
        return (act_rows[grid_row][chosen // RACT], act_cols[grid_col][chosen % RACT])
    total = ROWS_GRID * COLS_GRID
    left_rows, left_inner = jax.vmap(left_one)(jax.random.split(left_key, total), grid_rows)
    right_inner, right_cols = jax.vmap(right_one)(jax.random.split(right_key, total), grid_cols)
    result_rows, result_cols = jax.vmap(result_one)(jax.random.split(result_key, total), grid_rows, grid_cols)
    shaped = [left_rows, left_inner, right_inner, right_cols, result_rows, result_cols]
    return [jnp.reshape(entry, (ROWS_GRID, COLS_GRID, -1)).astype(jnp.int32) for entry in shaped]


def draw_a_rows(key, part):
    return pattern(key)[0]


def draw_a_inner(key, part):
    return pattern(key)[1]


def draw_b_inner(key, part):
    return pattern(key)[2]


def draw_b_cols(key, part):
    return pattern(key)[3]


def draw_c_rows(key, part):
    return pattern(key)[4]


def draw_c_cols(key, part):
    return pattern(key)[5]


def shard_levels(key, extent, pieces, low, top_value):
    factor_of, own = 1.0, jax.random.fold_in(key, 6)
    for position, blocks in pieces:
        draws = jnp.exp(jax.random.uniform(jax.random.fold_in(own, position), (blocks,), jnp.float32, low / len(pieces), top_value / len(pieces)))
        factor_of = factor_of * jnp.repeat(draws, extent[position] // blocks).reshape([-1 if axis == position else 1 for axis in range(len(extent))])
    return factor_of


def scatter_about(stream_key, shape, spread, most, pieces=(), kind=jnp.bfloat16):
    values = spread * jax.random.normal(stream_key, shape, jnp.float32)
    if pieces:
        values = values * shard_levels(stream_key, shape, pieces, -0.22, 0.18)
    return jnp.clip(values, -most, most).astype(kind)


def setup_inputs(seed: int = 0) -> dict:
    keys = jax.random.split(jax.random.key(seed), 9)
    return {
        "a_panels": scatter_about(keys[0], (ROWS_GRID, COLS_GRID, NBLK, BS, BS), 0.25, 1.5, ((0, 16), (1, 16))),
        "b_panels": scatter_about(keys[1], (ROWS_GRID, COLS_GRID, NBLK, BS, BS), 0.25, 1.5, ((0, 16), (1, 16))),
        "a_rows": draw_a_rows(jax.random.fold_in(keys[8], 71), 0),
        "a_inner": draw_a_inner(jax.random.fold_in(keys[8], 71), 0),
        "b_inner": draw_b_inner(jax.random.fold_in(keys[8], 71), 0),
        "b_cols": draw_b_cols(jax.random.fold_in(keys[8], 71), 0),
        "c_rows": draw_c_rows(jax.random.fold_in(keys[8], 71), 0),
        "c_cols": draw_c_cols(jax.random.fold_in(keys[8], 71), 0),
    }


def pick_pairs(left_inner, right_inner):
    count = right_inner.shape[0]
    places = jnp.arange(count, dtype=jnp.int32)
    matches = left_inner[:, None] == right_inner[None, :]
    first_pick = jnp.min(jnp.where(matches, places[None, :], count), axis=1)
    later = matches & (places[None, :] > first_pick[:, None])
    second_pick = jnp.min(jnp.where(later, places[None, :], count), axis=1)
    right_pick = jnp.stack([first_pick, second_pick], axis=1).reshape(-1).astype(jnp.int32)
    left_pick = jnp.repeat(jnp.arange(left_inner.shape[0], dtype=jnp.int32), 2)
    usable = right_pick < count
    return left_pick, jnp.minimum(right_pick, count - 1), usable


def target_slots(left_rows, right_cols, own_rows, own_cols, usable):
    slot_count = own_rows.shape[0]
    hit_table = (left_rows[:, None] == own_rows[None, :]) & (right_cols[:, None] == own_cols[None, :])
    places = jnp.arange(slot_count, dtype=jnp.int32)
    found_slot = jnp.min(jnp.where(hit_table, places[None, :], slot_count), axis=1)
    return jnp.where(usable, found_slot, slot_count).astype(jnp.int32)


def reference(a_panels, b_panels, a_rows, a_inner, b_inner, b_cols, c_rows, c_cols):
    def one_device(device):
        row_id = device // COLS_GRID
        col_id = device % COLS_GRID
        totals = jnp.zeros((NC, BS, BS), jnp.float32)
        for shift_step in range(STEPS):
            left_col = (col_id + shift_step) % COLS_GRID
            right_row = (row_id + shift_step) % ROWS_GRID
            left_blocks = a_panels[row_id, left_col]
            right_blocks = b_panels[right_row, col_id]
            left_pick, right_pick, usable = pick_pairs(a_inner[row_id, left_col], b_inner[right_row, col_id])
            slots = target_slots(a_rows[row_id, left_col][left_pick], b_cols[right_row, col_id][right_pick],
                                 c_rows[row_id, col_id], c_cols[row_id, col_id], usable)
            products = jnp.einsum("pik,pkj->pij", left_blocks[left_pick].astype(jnp.float32),
                                  right_blocks[right_pick].astype(jnp.float32))
            totals = totals.at[slots].add(products, mode="drop")
        return totals.astype(jnp.bfloat16)

    result = lax.map(one_device, jnp.arange(ROWS_GRID * COLS_GRID, dtype=jnp.int32))
    return result.reshape(ROWS_GRID, COLS_GRID, NC, BS, BS)
```

```python
import jax
import jax.numpy as jnp
import numpy as np
from jax import lax
from jax.experimental import pallas as pl
from jax.experimental.pallas import tpu as pltpu
from jax.sharding import PartitionSpec as P

STEPS = 4
MESH = pl.DeviceIdType.MESH

BLOCKS = 16
PLUS = 3
MAIN = BLOCKS - PLUS
MAIN_CHUNKS = [(at, min(2, MAIN - at)) for at in range(0, MAIN, 2)]
PLUS_CHUNKS = [(at, 1) for at in range(MAIN, BLOCKS)]
LEFT_CHUNKS = MAIN_CHUNKS + PLUS_CHUNKS
RIGHT_CHUNKS = [(at, 2) for at in range(0, BLOCKS, 2)]
N_MAIN, N_PLUS = len(MAIN_CHUNKS), len(PLUS_CHUNKS)
N_LEFT, N_RIGHT = len(LEFT_CHUNKS), len(RIGHT_CHUNKS)


def place():
    row_id, col_id = lax.axis_index("row"), lax.axis_index("col")
    return row_id // 8, (row_id // 2) % 4, row_id % 2, col_id // 2, col_id % 2


def device(x_lo, y, core, z, x_hi):
    return (x_lo * 8 + y * 2 + core, z * 2 + x_hi)


RUN = 2
RUNS = BLOCKS // RUN
GROUP = 2 * RUN
LAST_ORDER = (0, 1, 2, 3, 4, 5, 7, 6)
PRODUCTS = 2 * STEPS * BLOCKS
NONE = PRODUCTS


def order_table():
    rank = np.zeros(PRODUCTS, np.int32)
    for step in range(STEPS):
        for at in range(RUNS):
            run = LAST_ORDER[at] if step == STEPS - 1 else at
            for n in range(RUN):
                for t in range(2):
                    j = step * 2 * BLOCKS + t * BLOCKS + run * RUN + n
                    rank[j] = (step * RUNS + at) * GROUP + n * 2 + t
    return rank


def fill_tables(rows_ref, inner_ref, b_inner_ref, cols_ref, c_rows_ref, c_cols_ref, rank_row, rank_col, table, last):
    row, col = lax.axis_index("row"), lax.axis_index("col")
    i32 = jnp.int32
    down16 = lax.broadcasted_iota(i32, (BLOCKS, BLOCKS), 0)
    along16 = lax.broadcasted_iota(i32, (BLOCKS, BLOCKS), 1)

    def upright(values):
        spread = jnp.broadcast_to(values, (BLOCKS, BLOCKS))
        return jnp.sum(jnp.where(down16 == along16, spread, 0), axis=1, keepdims=True)

    picks, keys = [], []
    for step in range(STEPS):
        left_col, right_row = (col + step) % 16, (row + step) % 16
        inner = upright(inner_ref[row, pl.ds(left_col, 1), :])
        rows = upright(rows_ref[row, pl.ds(left_col, 1), :])
        b_inner = jnp.broadcast_to(b_inner_ref[right_row, pl.ds(col, 1), :], (BLOCKS, BLOCKS))
        b_cols = jnp.broadcast_to(cols_ref[right_row, pl.ds(col, 1), :], (BLOCKS, BLOCKS))
        match = inner == b_inner
        first = jnp.min(jnp.where(match, along16, BLOCKS), axis=1, keepdims=True)
        second = jnp.min(jnp.where(match & (along16 > first), along16, BLOCKS), axis=1, keepdims=True)
        for pick in (first, second):
            cols = jnp.sum(jnp.where(along16 == pick, b_cols, 0), axis=1, keepdims=True)
            picks.append(jnp.minimum(pick, BLOCKS - 1))
            keys.append(rows * 32 + cols)
    pick_col, key_col = jnp.concatenate(picks, axis=0), jnp.concatenate(keys, axis=0)
    square = (PRODUCTS, PRODUCTS)
    eye = lax.broadcasted_iota(i32, square, 0) == lax.broadcasted_iota(i32, square, 1)

    def level(values):
        return jnp.sum(jnp.where(eye, jnp.broadcast_to(values, square), 0), axis=0, keepdims=True)

    key_row = level(key_col)
    ranks = jnp.broadcast_to(rank_col[...], square)
    earlier = (jnp.broadcast_to(key_col, square) == key_row) & (ranks < rank_row[...])
    before = jnp.max(jnp.where(earlier, ranks, -1), axis=0, keepdims=True)
    table[0:1, :] = level(pick_col)
    table[1:2, :] = jnp.where(before < 0, NONE, before)
    slots = c_rows_ref.shape[2]
    slot_key = c_rows_ref[row, pl.ds(col, 1), :] * 32 + c_cols_ref[row, pl.ds(col, 1), :]
    tall = (PRODUCTS, slots)
    landed = jnp.broadcast_to(key_col, tall) == slot_key
    final = jnp.max(jnp.where(landed, jnp.broadcast_to(rank_col[...], tall), -1), axis=0, keepdims=True)
    last[...] = jnp.where(final < 0, NONE, final)


def gather_kernel(a_ref, b_ref, rows_ref, inner_ref, b_inner_ref, cols_ref, c_rows_ref, c_cols_ref, rank_row, rank_col,
                  partial, last,
                  a_own, b_own, j1, j2, j3, i1, i2, i3, q3, q6, relay, sums, stage, table, plain,
                  own_sem, table_sem, stage_sem,
                  s_j1, s_j2, s_j3, s_i1, s_i2, s_i2b, s_i3, s_q3, s_q6, s_rl, s_fw,
                  r_j1, r_j2, r_j3, r_i1, r_i2, r_i3, r_q3, r_q6, r_rl):
    x_lo, y, core, z, x_hi = place()
    own = a_ref.at[0, 0]
    own_b = b_ref.at[0, 0]
    even = y % 2 == 0
    wraps1 = (3 - y) // 3
    wraps2 = 1 - y // 2
    down = device(x_lo, y, core, (z + 7) % 8, x_hi)
    up = device(x_lo, y, core, (z + 1) % 8, x_hi)
    up3 = device(x_lo, y, core, (z + 3) % 8, x_hi)
    down3 = device(x_lo, y, core, (z + 5) % 8, x_hi)
    across = device(x_lo, y, core, z, 1 - x_hi)
    twin = device(x_lo, y, 1 - core, z, x_hi)
    prev1 = device((x_lo + wraps1) % 2, (y + 3) % 4, core, z, x_hi)
    after1 = device((x_lo + y // 3) % 2, (y + 1) % 4, core, z, x_hi)
    prev2 = device((x_lo + wraps2) % 2, (y + 2) % 4, 1 - core, z, x_hi)
    after2 = device((x_lo + y // 2) % 2, (y + 2) % 4, 1 - core, z, x_hi)
    wrap = device(x_lo, (y + 3) % 4, core, z, x_hi)
    next_y = device(x_lo, (y + 1) % 4, core, z, x_hi)
    beside = device(1 - x_lo, y, core, z, x_hi)

    barrier = pltpu.get_barrier_semaphore()
    others = (down, up, up3, down3, across, twin, prev1, after1, prev2, after2, wrap, next_y, beside)
    for other in others:
        pl.semaphore_signal(barrier, inc=1, device_id=other, device_id_type=MESH)
    pl.semaphore_wait(barrier, len(others))

    take_own = [
        pltpu.make_async_copy(own, a_own, own_sem.at[0]),
        pltpu.make_async_copy(own_b, b_own, own_sem.at[1]),
    ]

    def part(ref, chunk, shift=0):
        return ref.at[pl.ds(chunk[0] - shift, chunk[1])]

    def send(src, dst, s_sem, r_sem, to):
        return pltpu.make_async_remote_copy(
            src_ref=src, dst_ref=dst, send_sem=s_sem, recv_sem=r_sem, device_id=to, device_id_type=MESH
        )

    def to_j2(k, src, to):
        return send(src, part(j2, LEFT_CHUNKS[k]), s_j2.at[k], r_j2.at[k], to)

    def to_j1(k, src):
        return send(part(src, LEFT_CHUNKS[k]), part(j1, LEFT_CHUNKS[k]), s_j1.at[k], r_j1.at[k], across)

    def to_j3(k, src, to):
        return send(src, part(j3, LEFT_CHUNKS[k]), s_j3.at[k], r_j3.at[k], to)

    def to_q3(k):
        chunk = PLUS_CHUNKS[k]
        return send(part(own, chunk), part(q3, chunk, MAIN), s_q3.at[k], r_q3.at[k], up3)

    def to_q6(k):
        chunk = PLUS_CHUNKS[k]
        return send(part(q3, chunk, MAIN), part(q6, chunk, MAIN), s_q6.at[k], r_q6.at[k], up3)

    def to_right(k, src, dst, s_sem, r_sem, to):
        return send(part(src, RIGHT_CHUNKS[k]), part(dst, RIGHT_CHUNKS[k]), s_sem.at[k], r_sem.at[k], to)

    for k in range(N_PLUS):
        to_q3(k).start()
    for k in range(max(N_MAIN, N_RIGHT)):
        if k < N_MAIN:
            to_j2(k, part(own, LEFT_CHUNKS[k]), down).start()

            @pl.when(x_hi == 1)
            def _():
                to_j1(k, own).start()

        if k < N_RIGHT:

            @pl.when(core == 0)
            def _():
                @pl.when(y % 2 == 1)
                def _():
                    to_right(k, own_b, i2, s_i2b, r_i2, prev1).start()

                @pl.when(y % 2 == 0)
                def _():
                    to_right(k, own_b, i3, s_i3, r_i3, prev2).start()

            @pl.when(core == 1)
            def _():
                to_right(k, own_b, i1, s_i1, r_i1, twin).start()

                @pl.when(y == 0)
                def _():
                    to_right(k, own_b, relay, s_rl, r_rl, wrap).start()

                @pl.when(y != 0)
                def _():
                    to_right(k, own_b, i2, s_i2, r_i2, prev1).start()

    @pl.when(x_hi == 1)
    def _():
        for k in range(N_MAIN, N_LEFT):
            to_j1(k, own).start()

    @pl.when((core == 0) & (y % 2 == 1))
    def _():
        for k in range(N_RIGHT):
            to_right(k, own_b, i3, s_i3, r_i3, prev2).start()

    for copy in take_own:
        copy.start()
    fill_tables(rows_ref, inner_ref, b_inner_ref, cols_ref, c_rows_ref, c_cols_ref, rank_row, rank_col, table, last)
    to_plain = pltpu.make_async_copy(table, plain, table_sem)
    to_plain.start()
    sums[NONE] = jnp.zeros(sums.shape[1:], sums.dtype)
    stage[...] = jnp.zeros(stage.shape, stage.dtype)

    def put(group):
        return pltpu.make_async_copy(
            stage.at[group % 2], partial.at[pl.ds(group * GROUP, GROUP)], stage_sem.at[group % 2]
        )

    for n in range(2):
        put(PRODUCTS // GROUP + n).start()
    to_plain.wait()

    def on_j2(k):
        to_j2(k, part(own, LEFT_CHUNKS[k]), down).wait_recv()

        @pl.when(x_hi == 0)
        def _():
            to_j1(k, j2).start()

        if k >= N_MAIN:

            @pl.when(x_hi == 1)
            def _():
                to_j3(k, part(j2, LEFT_CHUNKS[k]), across).start()

    def on_j1(k):
        to_j1(k, own).wait_recv()
        if k < N_MAIN:
            to_j3(k, part(j1, LEFT_CHUNKS[k]), down).start()

    def on_j3(k):
        to_j3(k, part(j1, LEFT_CHUNKS[k]), down).wait_recv()

    def on_q3(k):
        to_q3(k).wait_recv()
        to_q6(k).start()

    def on_q6(k):
        to_q6(k).wait_recv()
        mine = part(q6, PLUS_CHUNKS[k], MAIN)
        to_j2(N_MAIN + k, mine, up).start()

        @pl.when(x_hi == 0)
        def _():
            to_j3(N_MAIN + k, mine, across).start()

    def on_i1(k):
        to_right(k, own_b, i1, s_i1, r_i1, twin).wait_recv()

        @pl.when((core == 1) & (y % 2 == 1))
        def _():
            to_right(k, i1, i2, s_i2b, r_i2, twin).start()

    def on_i2(k):
        to_right(k, own_b, i2, s_i2, r_i2, prev1).wait_recv()

        @pl.when(core == 1)
        def _():
            to_right(k, i2, i3, s_i3, r_i3, twin).start()

        @pl.when((core == 0) & (y % 2 == 0))
        def _():
            to_right(k, i2, i1, s_i1, r_i1, twin).start()

    def on_i3(k):
        to_right(k, own_b, i3, s_i3, r_i3, prev2).wait_recv()

        @pl.when((core == 1) & (y % 2 == 0))
        def _():
            to_right(k, i3, i1, s_fw, r_i1, next_y).start()

    def on_relay(k):
        @pl.when((core == 1) & (y == 3))
        def _():
            to_right(k, own_b, relay, s_rl, r_rl, wrap).wait_recv()
            to_right(k, relay, i2, s_fw, r_i2, beside).start()

    lefts, rights = (a_own, j1, j2, j3), (b_own, i1, i2, i3)

    def multiply_run(step, run, group):
        put(group).wait()
        for n in range(RUN):
            block = lefts[step][run * RUN + n]
            for t in range(2):
                j = step * 2 * BLOCKS + t * BLOCKS + run * RUN + n
                rank = group * GROUP + 2 * n + t
                total = sums[plain[1, j]] + jnp.dot(
                    block, rights[step][plain[0, j]], preferred_element_type=jnp.float32
                )
                sums[rank] = total
                stage[group % 2, 2 * n + t] = total.astype(stage.dtype)
        put(group).start()

    def multiply(step, first, count):
        if count == 1:
            run = LAST_ORDER[first] if step == STEPS - 1 else first
            multiply_run(step, run, step * RUNS + first)
        else:

            @pl.loop(first, first + count)
            def _(run):
                multiply_run(step, run, step * RUNS + run)

    for event in schedule():
        kind, arg = event[0], event[1:]
        if kind == "own":
            for copy in take_own:
                copy.wait()
        elif kind == "x":
            multiply(*arg)
        else:
            {"j1": on_j1, "j2": on_j2, "j3": on_j3, "q3": on_q3, "q6": on_q6,
             "i1": on_i1, "i2": on_i2, "i3": on_i3, "rl": on_relay}[kind](*arg)
    for group in range(2):
        put(group).wait()

    for k in range(N_LEFT):
        chunk = LEFT_CHUNKS[k]
        to_j2(k, part(own, chunk), down).wait_send()
        to_j1(k, own).wait_send()
        to_j3(k, part(own, chunk), down).wait_send()
    for k in range(N_PLUS):
        to_q3(k).wait_send()
        to_q6(k).wait_send()
    for k in range(N_RIGHT):
        to_right(k, own_b, i3, s_i3, r_i3, twin).wait_send()

        @pl.when((core == 1) | even)
        def _():
            to_right(k, own_b, i1, s_i1, r_i1, twin).wait_send()

        @pl.when(y % 2 == 1)
        def _():
            to_right(k, own_b, i2, s_i2b, r_i2, twin).wait_send()

        @pl.when((core == 1) & (y != 0))
        def _():
            to_right(k, own_b, i2, s_i2, r_i2, prev1).wait_send()

        @pl.when((core == 1) & (y != 1))
        def _():
            to_right(k, own_b, i1, s_fw, r_i1, next_y).wait_send()

        @pl.when((core == 1) & (y == 0))
        def _():
            to_right(k, own_b, relay, s_rl, r_rl, wrap).wait_send()


def schedule():
    timed = [(1, "own"), (4.5, "x", 0, 0, RUNS)]
    for k in range(N_MAIN):
        timed += [(5.4 * (k + 1) + 2, "j2", k), (16 + 5.4 * (k + 1), "j1", k), (46 + 5 * (k + 1), "j3", k)]
    for k in range(N_PLUS):
        timed += [
            (8.6 * (k + 1) + 2, "q3", k),
            (12 + 17 * (k + 1), "q6", k),
            (18 + 17 * (k + 1), "j2", N_MAIN + k),
            (24 + 17 * (k + 1), "j1", N_MAIN + k),
            (75 + k, "j3", N_MAIN + k),
        ]
    for k in range(N_RIGHT):
        timed += [
            (5.5 * (k + 1) + 2, "rl", k),
            (8.5 * (k + 1) + 2, "i3", k),
            (56 + 0.1 * k, "i2", k),
            (59 + 0.1 * k, "i1", k),
        ]
    timed.sort(key=lambda event: event[0])
    events = [event[1:] for event in timed]
    todo = [(1, 0, RUNS), (2, 0, RUNS), (3, 0, 4), (3, 4, 1), (3, 5, 1), (3, 6, 1), (3, 7, 1)]
    done, out = set(), []

    def needs(step, first, count):
        places = range(first, first + count)
        runs = [LAST_ORDER[at] if step == STEPS - 1 else at for at in places]
        blocks = {run * RUN + n for run in runs for n in range(RUN)}
        chunks = {k for k, (at, n) in enumerate(LEFT_CHUNKS) if blocks & set(range(at, at + n))}
        return {(f"j{step}", k) for k in chunks} | {(f"i{step}", k) for k in range(N_RIGHT)}

    for event in events:
        out.append(event)
        done.add(event)
        while todo and needs(*todo[0]) <= done:
            out.append(("x", *todo.pop(0)))
    return out


def gather(a_panels, b_panels, indices):
    dtype = a_panels.dtype
    tail = a_panels.shape[3:]
    slots = indices[-1].shape[2]
    rank = order_table()
    anywhere = pl.BlockSpec(memory_space=pl.ANY)
    in_vmem = pl.BlockSpec(memory_space=pltpu.VMEM)
    sems = [2, 1, 2]
    sems += [N_LEFT] * 3 + [N_RIGHT] * 4 + [N_PLUS] * 2 + [N_RIGHT] * 2
    sems += [N_LEFT] * 3 + [N_RIGHT] * 3 + [N_PLUS] * 2 + [N_RIGHT]
    scratch = [pltpu.VMEM((BLOCKS, *tail), dtype)] * 8 + [pltpu.VMEM((PLUS, *tail), dtype)] * 2
    scratch += [
        pltpu.VMEM((BLOCKS, *tail), dtype),
        pltpu.VMEM((PRODUCTS + 1, *tail), jnp.float32),
        pltpu.VMEM((2, GROUP, *tail), dtype),
        pltpu.VMEM((8, PRODUCTS), jnp.int32),
        pltpu.SMEM((8, PRODUCTS), jnp.int32),
    ]
    return pl.pallas_call(
        gather_kernel,
        out_shape=[
            jax.ShapeDtypeStruct((PRODUCTS + 2 * GROUP, *tail), dtype),
            jax.ShapeDtypeStruct((1, slots), jnp.int32),
        ],
        in_specs=[anywhere] * 2 + [in_vmem] * 8,
        out_specs=[anywhere, in_vmem],
        scratch_shapes=scratch + [pltpu.SemaphoreType.DMA((n,)) if n > 1 else pltpu.SemaphoreType.DMA for n in sems],
        compiler_params=pltpu.CompilerParams(collective_id=0, has_side_effects=True, vmem_limit_bytes=67000000),
        name="gather",
    )(a_panels, b_panels, *indices, jnp.asarray(rank)[None, :], jnp.asarray(rank)[:, None])


def place_kernel(last, partial, out, stage, in_sem, out_sem):
    count = stage.shape[0]

    def fetch(n):
        return pltpu.make_async_copy(partial.at[last[0, n]], stage.at[n], in_sem.at[n])

    def put(n):
        return pltpu.make_async_copy(stage.at[n], out.at[0, 0, n], out_sem.at[n])

    @pl.loop(0, count)
    def _(n):
        fetch(n).start()

    @pl.loop(0, count)
    def _(n):
        fetch(n).wait()
        put(n).start()

    @pl.loop(0, count)
    def _(n):
        put(n).wait()


def on_device(a_panels, b_panels, a_rows, a_inner, b_inner, b_cols, c_rows, c_cols):
    partial, last = gather(a_panels, b_panels, (a_rows, a_inner, b_inner, b_cols, c_rows, c_cols))
    slots, width = c_rows.shape[2], a_panels.shape[3]
    anywhere = pl.BlockSpec(memory_space=pl.ANY)
    return pl.pallas_call(
        place_kernel,
        out_shape=jax.ShapeDtypeStruct((1, 1, slots, width, width), a_panels.dtype),
        grid_spec=pltpu.PrefetchScalarGridSpec(
            num_scalar_prefetch=1,
            grid=(),
            in_specs=[anywhere],
            out_specs=anywhere,
            scratch_shapes=[
                pltpu.VMEM((slots, width, width), a_panels.dtype),
                pltpu.SemaphoreType.DMA((slots,)),
                pltpu.SemaphoreType.DMA((slots,)),
            ],
        ),
        name="place",
    )(last, partial)


def solution(mesh):
    in_specs = (
        P("row", "col", None, None, None),
        P("row", "col", None, None, None),
        P(),
        P(),
        P(),
        P(),
        P(),
        P(),
    )
    out_specs = P("row", "col", None, None, None)
    return jax.shard_map(
        on_device, mesh=mesh, in_specs=in_specs, out_specs=out_specs, check_vma=False
    )
```

```python
import jax
import jax.numpy as jnp
import numpy as np
from jax import lax
from jax.experimental import pallas as pl
from jax.experimental.pallas import tpu as pltpu
from jax.sharding import PartitionSpec as P

STEPS = 4
MESH = pl.DeviceIdType.MESH

BLOCKS = 16
PLUS = 3
MAIN = BLOCKS - PLUS
MAIN_CHUNKS = [(at, min(2, MAIN - at)) for at in range(0, MAIN, 2)]
PLUS_CHUNKS = [(at, 1) for at in range(MAIN, BLOCKS)]
LEFT_CHUNKS = MAIN_CHUNKS + PLUS_CHUNKS
RIGHT_CHUNKS = [(at, 2) for at in range(0, BLOCKS, 2)]
N_MAIN, N_PLUS = len(MAIN_CHUNKS), len(PLUS_CHUNKS)
N_LEFT, N_RIGHT = len(LEFT_CHUNKS), len(RIGHT_CHUNKS)


def place():
    row_id, col_id = lax.axis_index("row"), lax.axis_index("col")
    return row_id // 8, (row_id // 2) % 4, row_id % 2, col_id // 2, col_id % 2


def device(x_lo, y, core, z, x_hi):
    return (x_lo * 8 + y * 2 + core, z * 2 + x_hi)


LEAD = 1
CROSS_AT = (-1, -1, -1, 3)
HALF = N_RIGHT // 2
RUN = 2
RUNS = BLOCKS // RUN
GROUP = 2 * RUN
PRODUCTS = 2 * STEPS * BLOCKS
NONE = PRODUCTS
PIECES = ((0, 0, RUNS), (1, 0, 6), (3, 0, 2), (2, 0, 6), (3, 4, 1), (3, 3, 1), (3, 2, 1), (2, 6, 1), (2, 7, 1), (3, 5, 1), (1, 6, 1), (1, 7, 1), (3, 6, 1), (3, 7, 1))
ORDERS = (
(
    ("rl", 0), ("j2", 0), ("rl", 4), ("j1", 0), ("q3", 0), ("rl", 5), ("j2", 1), ("q3", 1), ("rl", 1), ("rl", 7),
    ("rl", 6), ("j2", 2), ("q3", 2), ("j1", 2), ("j2", 3), ("rl", 2), ("i2", 0), ("rl", 3), ("j2", 4), ("j1", 1),
    ("i2", 1), ("j2", 5), ("i3", 0), ("i1", 0), ("j2", 6), ("j1", 3), ("i2", 5), ("i2", 4), ("i3", 1), ("i1", 1),
    ("i3", 4), ("i1", 4), ("q6", 1), ("q6", 0), ("j1", 4), ("q6", 2), ("i2", 6), ("i3", 5), ("i1", 5), ("j2", 8),
    ("j3", 1), ("i2", 7), ("i2", 2), ("i3", 2), ("i1", 2), ("j2", 7), ("i3", 6), ("i1", 6), ("i2", 3), ("j3", 0),
    ("i3", 7), ("i1", 7), ("j2", 9), ("j1", 5), ("j1", 6), ("j3", 2), ("i3", 3), ("i1", 3), ("j3", 3), ("j3", 4),
    ("j1", 7), ("j3", 7), ("j3", 5), ("j1", 8), ("j3", 8), ("j3", 6), ("j1", 9), ("j3", 9),
),
)


def order_table():
    rank = np.zeros(PRODUCTS, np.int32)
    at = 0
    for step, first, count in PIECES:
        for block in range(first * RUN, (first + count) * RUN):
            for t in range(2):
                rank[step * 2 * BLOCKS + t * BLOCKS + block] = at
                at += 1
    return rank


def fill_tables(rows_ref, inner_ref, b_inner_ref, cols_ref, c_rows_ref, c_cols_ref, rank_row, rank_col, table, last):
    row, col = lax.axis_index("row"), lax.axis_index("col")
    i32 = jnp.int32
    down16 = lax.broadcasted_iota(i32, (BLOCKS, BLOCKS), 0)
    along16 = lax.broadcasted_iota(i32, (BLOCKS, BLOCKS), 1)

    def upright(values):
        spread = jnp.broadcast_to(values, (BLOCKS, BLOCKS))
        return jnp.sum(jnp.where(down16 == along16, spread, 0), axis=1, keepdims=True)

    picks, keys = [], []
    for step in range(STEPS):
        left_col, right_row = (col + step) % 16, (row + step) % 16
        inner = upright(inner_ref[row, pl.ds(left_col, 1), :])
        rows = upright(rows_ref[row, pl.ds(left_col, 1), :])
        b_inner = jnp.broadcast_to(b_inner_ref[right_row, pl.ds(col, 1), :], (BLOCKS, BLOCKS))
        b_cols = jnp.broadcast_to(cols_ref[right_row, pl.ds(col, 1), :], (BLOCKS, BLOCKS))
        match = inner == b_inner
        first = jnp.min(jnp.where(match, along16, BLOCKS), axis=1, keepdims=True)
        second = jnp.min(jnp.where(match & (along16 > first), along16, BLOCKS), axis=1, keepdims=True)
        for pick in (first, second):
            cols = jnp.sum(jnp.where(along16 == pick, b_cols, 0), axis=1, keepdims=True)
            picks.append(jnp.minimum(pick, BLOCKS - 1))
            keys.append(rows * 32 + cols)
    pick_col, key_col = jnp.concatenate(picks, axis=0), jnp.concatenate(keys, axis=0)
    square = (PRODUCTS, PRODUCTS)
    eye = lax.broadcasted_iota(i32, square, 0) == lax.broadcasted_iota(i32, square, 1)

    def level(values):
        return jnp.sum(jnp.where(eye, jnp.broadcast_to(values, square), 0), axis=0, keepdims=True)

    key_row = level(key_col)
    ranks = jnp.broadcast_to(rank_col[...], square)
    earlier = (jnp.broadcast_to(key_col, square) == key_row) & (ranks < rank_row[...])
    before = jnp.max(jnp.where(earlier, ranks, -1), axis=0, keepdims=True)
    table[0:1, :] = level(pick_col)
    table[1:2, :] = jnp.where(before < 0, NONE, before)
    slots = c_rows_ref.shape[2]
    slot_key = c_rows_ref[row, pl.ds(col, 1), :] * 32 + c_cols_ref[row, pl.ds(col, 1), :]
    tall = (PRODUCTS, slots)
    landed = jnp.broadcast_to(key_col, tall) == slot_key
    final = jnp.max(jnp.where(landed, jnp.broadcast_to(rank_col[...], tall), -1), axis=0, keepdims=True)
    last[...] = jnp.where(final < 0, NONE, final)


def gather_kernel(a_ref, b_ref, rows_ref, inner_ref, b_inner_ref, cols_ref, c_rows_ref, c_cols_ref, rank_row, rank_col,
                  partial, last,
                  a_own, b_own, j1, j2, j3, i1, i2, i3, q3, q6, relay, sums, stage, table, plain,
                  own_sem, table_sem, stage_sem,
                  s_j1, s_j2, s_j3, s_i1, s_i2, s_i2b, s_i3, s_q3, s_q6, s_rl, s_fw, s_x,
                  r_j1, r_j2, r_j3, r_i1, r_i2, r_i3, r_q3, r_q6, r_rl):
    x_lo, y, core, z, x_hi = place()
    own = a_ref.at[0, 0]
    own_b = b_ref.at[0, 0]
    even = y % 2 == 0
    wraps1 = (3 - y) // 3
    wraps2 = 1 - y // 2
    down = device(x_lo, y, core, (z + 7) % 8, x_hi)
    up = device(x_lo, y, core, (z + 1) % 8, x_hi)
    up3 = device(x_lo, y, core, (z + 3) % 8, x_hi)
    down3 = device(x_lo, y, core, (z + 5) % 8, x_hi)
    across = device(x_lo, y, core, z, 1 - x_hi)
    twin = device(x_lo, y, 1 - core, z, x_hi)
    prev1 = device((x_lo + wraps1) % 2, (y + 3) % 4, core, z, x_hi)
    after1 = device((x_lo + y // 3) % 2, (y + 1) % 4, core, z, x_hi)
    prev2 = device((x_lo + wraps2) % 2, (y + 2) % 4, 1 - core, z, x_hi)
    after2 = device((x_lo + y // 2) % 2, (y + 2) % 4, 1 - core, z, x_hi)
    wrap = device(x_lo, (y + 3) % 4, core, z, x_hi)
    next_y = device(x_lo, (y + 1) % 4, core, z, x_hi)
    beside = device(1 - x_lo, y, core, z, x_hi)

    barrier = pltpu.get_barrier_semaphore()
    apart = device(x_lo, (y + 2) % 4, 1 - core, z, x_hi)
    beside_twin = device(1 - x_lo, y, 1 - core, z, x_hi)
    wrap_twin = device(x_lo, (y + 3) % 4, 1 - core, z, x_hi)
    next_twin = device(x_lo, (y + 1) % 4, 1 - core, z, x_hi)
    prev2_same = device((x_lo + wraps2) % 2, (y + 2) % 4, core, z, x_hi)
    after2_same = device((x_lo + y // 2) % 2, (y + 2) % 4, core, z, x_hi)
    others = (
        down, up, up3, down3, across, twin, prev1, after1, prev2, after2, wrap, next_y, beside,
        apart, beside_twin, wrap_twin, next_twin, prev2_same, after2_same,
    )
    for other in others:
        pl.semaphore_signal(barrier, inc=1, device_id=other, device_id_type=MESH)
    pl.semaphore_wait(barrier, len(others))

    take_own = [
        pltpu.make_async_copy(own, a_own, own_sem.at[0]),
        pltpu.make_async_copy(own_b, b_own, own_sem.at[1]),
    ]

    def part(ref, chunk, shift=0):
        return ref.at[pl.ds(chunk[0] - shift, chunk[1])]

    def send(src, dst, s_sem, r_sem, to):
        return pltpu.make_async_remote_copy(
            src_ref=src, dst_ref=dst, send_sem=s_sem, recv_sem=r_sem, device_id=to, device_id_type=MESH
        )

    def to_j2(k, src, to):
        return send(src, part(j2, LEFT_CHUNKS[k]), s_j2.at[k], r_j2.at[k], to)

    def to_j1(k, src):
        return send(part(src, LEFT_CHUNKS[k]), part(j1, LEFT_CHUNKS[k]), s_j1.at[k], r_j1.at[k], across)

    def to_j3(k, src, to):
        return send(src, part(j3, LEFT_CHUNKS[k]), s_j3.at[k], r_j3.at[k], to)

    def to_q3(k):
        chunk = PLUS_CHUNKS[k]
        return send(part(own, chunk), part(q3, chunk, MAIN), s_q3.at[k], r_q3.at[k], up3)

    def to_q6(k):
        chunk = PLUS_CHUNKS[k]
        return send(part(q3, chunk, MAIN), part(q6, chunk, MAIN), s_q6.at[k], r_q6.at[k], up3)

    def to_right(k, src, dst, s_sem, r_sem, to):
        return send(part(src, RIGHT_CHUNKS[k]), part(dst, RIGHT_CHUNKS[k]), s_sem.at[k], r_sem.at[k], to)

    def cross(k):
        @pl.when((core == 0) & (y == 0))
        def _():
            to_right(k, own_b, i3, s_i3, r_i3, prev2).start()

        @pl.when((core == 0) & (y == 1))
        def _():
            to_right(k, own_b, relay, s_rl, r_rl, beside).start()

    for k in range(N_PLUS):
        to_q3(k).start()
    for k in range(max(N_MAIN, N_RIGHT)):
        if k < N_MAIN:
            to_j2(k, part(own, LEFT_CHUNKS[k]), down).start()
        if k < LEAD:

            @pl.when(x_hi == 1)
            def _():
                to_j1(k, own).start()

        if k < N_RIGHT:

            @pl.when(core == 0)
            def _():
                @pl.when(y % 2 == 1)
                def _():
                    to_right(k, own_b, i2, s_i2b, r_i2, prev1).start()

                @pl.when(y == 2)
                def _():
                    to_right(k, own_b, i3, s_i3, r_i3, prev2).start()

                if k >= HALF:

                    @pl.when(y < 2)
                    def _():
                        to_right(k, own_b, relay, s_rl, r_rl, twin).start()

            @pl.when(core == 1)
            def _():
                to_right(k, own_b, i1, s_i1, r_i1, twin).start()

                @pl.when(y == 0)
                def _():
                    to_right(k, own_b, relay, s_rl, r_rl, wrap if k < HALF else wrap_twin).start()

                @pl.when(y != 0)
                def _():
                    to_right(k, own_b, i2, s_i2, r_i2, prev1).start()

    @pl.when((core == 0) & (y == 3))
    def _():
        for k in range(N_RIGHT):
            to_right(k, own_b, i3, s_i3, r_i3, prev2).start()

    for k in range(HALF):
        if CROSS_AT[k] < 0:
            cross(k)

    for copy in take_own:
        copy.start()
    fill_tables(rows_ref, inner_ref, b_inner_ref, cols_ref, c_rows_ref, c_cols_ref, rank_row, rank_col, table, last)
    to_plain = pltpu.make_async_copy(table, plain, table_sem)
    to_plain.start()
    sums[NONE] = jnp.zeros(sums.shape[1:], sums.dtype)
    stage[...] = jnp.zeros(stage.shape, stage.dtype)

    def put(group):
        return pltpu.make_async_copy(
            stage.at[group % 2], partial.at[pl.ds(group * GROUP, GROUP)], stage_sem.at[group % 2]
        )

    for n in range(2):
        put(PRODUCTS // GROUP + n).start()
    to_plain.wait()

    def on_j2(k):
        to_j2(k, part(own, LEFT_CHUNKS[k]), down).wait_recv()

        @pl.when(x_hi == 0)
        def _():
            to_j1(k, j2).start()

        if k + LEAD < N_LEFT:

            @pl.when(x_hi == 1)
            def _():
                to_j1(k + LEAD, own).start()

        if k >= N_MAIN:

            @pl.when(x_hi == 1)
            def _():
                to_j3(k, part(j2, LEFT_CHUNKS[k]), across).start()

        for n in range(HALF):
            if CROSS_AT[n] == k:
                cross(n)

    def on_j1(k):
        to_j1(k, own).wait_recv()
        if k < N_MAIN:
            to_j3(k, part(j1, LEFT_CHUNKS[k]), down).start()

    def on_j3(k):
        to_j3(k, part(j1, LEFT_CHUNKS[k]), down).wait_recv()

    def on_q3(k):
        to_q3(k).wait_recv()
        to_q6(k).start()

    def on_q6(k):
        to_q6(k).wait_recv()
        mine = part(q6, PLUS_CHUNKS[k], MAIN)
        to_j2(N_MAIN + k, mine, up).start()

        @pl.when(x_hi == 0)
        def _():
            to_j3(N_MAIN + k, mine, across).start()

    def on_i1(k):
        to_right(k, own_b, i1, s_i1, r_i1, twin).wait_recv()

        @pl.when((core == 1) & (y % 2 == 1))
        def _():
            to_right(k, i1, i2, s_i2b, r_i2, twin).start()

    def on_i2(k):
        to_right(k, own_b, i2, s_i2, r_i2, prev1).wait_recv()

        @pl.when(core == 1)
        def _():
            to_right(k, i2, i3, s_i3, r_i3, twin).start()

        @pl.when((core == 0) & (y % 2 == 0))
        def _():
            to_right(k, i2, i1, s_i1, r_i1, twin).start()

    def on_i3(k):
        to_right(k, own_b, i3, s_i3, r_i3, prev2).wait_recv()

        @pl.when((core == 1) & (y % 2 == 0))
        def _():
            to_right(k, i3, i1, s_fw, r_i1, next_y).start()

    def on_relay(k):
        arrived = to_right(k, own_b, relay, s_rl, r_rl, wrap)
        if k >= HALF:

            @pl.when((core == 1) & (y == 0))
            def _():
                arrived.wait_recv()
                to_right(k, relay, i3, s_x, r_i3, prev2_same).start()

            @pl.when((core == 1) & (y == 1))
            def _():
                arrived.wait_recv()
                to_right(k, relay, relay, s_x, r_rl, beside_twin).start()

        @pl.when((core == 0) & (y == 1))
        def _():
            arrived.wait_recv()
            to_right(k, relay, i3, s_i3, r_i3, apart).start()

        @pl.when((core == (1 if k < HALF else 0)) & (y == 3))
        def _():
            arrived.wait_recv()
            to_right(k, relay, i2, s_x, r_i2, beside if k < HALF else beside_twin).start()

    lefts, rights = (a_own, j1, j2, j3), (b_own, i1, i2, i3)

    def multiply_run(step, run, group):
        put(group).wait()
        for n in range(RUN):
            block = lefts[step][run * RUN + n]
            for t in range(2):
                j = step * 2 * BLOCKS + t * BLOCKS + run * RUN + n
                rank = group * GROUP + 2 * n + t
                total = sums[plain[1, j]] + jnp.dot(
                    block, rights[step][plain[0, j]], preferred_element_type=jnp.float32
                )
                sums[rank] = total
                stage[group % 2, 2 * n + t] = total.astype(stage.dtype)
        put(group).start()

    def multiply(step, first, count, group):
        if count == 1:
            multiply_run(step, first, group)
        else:

            @pl.loop(0, count)
            def _(n):
                multiply_run(step, first + n, group + n)

    handlers = {
        "j1": on_j1, "j2": on_j2, "j3": on_j3, "q3": on_q3, "q6": on_q6,
        "i1": on_i1, "i2": on_i2, "i3": on_i3, "rl": on_relay,
    }

    for copy in take_own:
        copy.wait()
    multiply(*PIECES[0], 0)

    def follow(order):
        for event in with_products(order):
            if event[0] == "x":
                multiply(*event[1:])
            else:
                handlers[event[0]](event[1])

    if len(ORDERS) == 1:
        follow(ORDERS[0])
    else:
        for which, order in enumerate(ORDERS):

            @pl.when(core == which)
            def _():
                follow(order)

    for group in range(2):
        put(group).wait()

    for k in range(N_LEFT):
        chunk = LEFT_CHUNKS[k]
        to_j2(k, part(own, chunk), down).wait_send()
        to_j1(k, own).wait_send()
        to_j3(k, part(own, chunk), down).wait_send()
    for k in range(N_PLUS):
        to_q3(k).wait_send()
        to_q6(k).wait_send()
    for k in range(N_RIGHT):
        first_half = k < HALF

        @pl.when((core == 1) | (y != 0) | first_half)
        def _():
            to_right(k, own_b, i3, s_i3, r_i3, twin).wait_send()

        @pl.when((core == 1) | even)
        def _():
            to_right(k, own_b, i1, s_i1, r_i1, twin).wait_send()

        @pl.when(y % 2 == 1)
        def _():
            to_right(k, own_b, i2, s_i2b, r_i2, twin).wait_send()

        @pl.when((core == 1) & (y != 0))
        def _():
            to_right(k, own_b, i2, s_i2, r_i2, prev1).wait_send()

        @pl.when((core == 1) & even)
        def _():
            to_right(k, own_b, i1, s_fw, r_i1, next_y).wait_send()

        if first_half:
            staged, passed = ((core == 0) & (y == 1)) | ((core == 1) & (y == 0)), (core == 1) & (y == 3)
        else:
            staged = ((core == 0) & (y < 2)) | ((core == 1) & (y == 0))
            passed = ((core == 1) & (y < 2)) | ((core == 0) & (y == 3))

        @pl.when(staged)
        def _():
            to_right(k, own_b, relay, s_rl, r_rl, wrap).wait_send()

        @pl.when(passed)
        def _():
            to_right(k, own_b, relay, s_x, r_rl, wrap).wait_send()


def with_products(order):
    todo, group = [], RUNS
    for step, first, count in PIECES[1:]:
        blocks = set(range(first * RUN, (first + count) * RUN))
        chunks = {k for k, (at, n) in enumerate(LEFT_CHUNKS) if blocks & set(range(at, at + n))}
        needs = {(f"j{step}", k) for k in chunks} | {(f"i{step}", k) for k in range(N_RIGHT)}
        todo.append((needs, ("x", step, first, count, group)))
        group += count
    done, out = set(), []
    for event in order:
        out.append(event)
        done.add(event)
        while todo and todo[0][0] <= done:
            out.append(todo.pop(0)[1])
    return out


def gather(a_panels, b_panels, indices):
    dtype = a_panels.dtype
    tail = a_panels.shape[3:]
    slots = indices[-1].shape[2]
    rank = order_table()
    anywhere = pl.BlockSpec(memory_space=pl.ANY)
    in_vmem = pl.BlockSpec(memory_space=pltpu.VMEM)
    sems = [2, 1, 2]
    sems += [N_LEFT] * 3 + [N_RIGHT] * 4 + [N_PLUS] * 2 + [N_RIGHT] * 3
    sems += [N_LEFT] * 3 + [N_RIGHT] * 3 + [N_PLUS] * 2 + [N_RIGHT]
    scratch = [pltpu.VMEM((BLOCKS, *tail), dtype)] * 8 + [pltpu.VMEM((PLUS, *tail), dtype)] * 2
    scratch += [
        pltpu.VMEM((BLOCKS, *tail), dtype),
        pltpu.VMEM((PRODUCTS + 1, *tail), jnp.float32),
        pltpu.VMEM((2, GROUP, *tail), dtype),
        pltpu.VMEM((8, PRODUCTS), jnp.int32),
        pltpu.SMEM((8, PRODUCTS), jnp.int32),
    ]
    return pl.pallas_call(
        gather_kernel,
        out_shape=[
            jax.ShapeDtypeStruct((PRODUCTS + 2 * GROUP, *tail), dtype),
            jax.ShapeDtypeStruct((1, slots), jnp.int32),
        ],
        in_specs=[anywhere] * 2 + [in_vmem] * 8,
        out_specs=[anywhere, in_vmem],
        scratch_shapes=scratch + [pltpu.SemaphoreType.DMA((n,)) if n > 1 else pltpu.SemaphoreType.DMA for n in sems],
        compiler_params=pltpu.CompilerParams(collective_id=0, has_side_effects=True, vmem_limit_bytes=67000000),
        name="gather",
    )(a_panels, b_panels, *indices, jnp.asarray(rank)[None, :], jnp.asarray(rank)[:, None])


def place_kernel(last, partial, out, stage, in_sem, out_sem):
    count = stage.shape[0]

    def fetch(n):
        return pltpu.make_async_copy(partial.at[last[0, n]], stage.at[n], in_sem.at[n])

    def put(n):
        return pltpu.make_async_copy(stage.at[n], out.at[0, 0, n], out_sem.at[n])

    @pl.loop(0, count)
    def _(n):
        fetch(n).start()

    @pl.loop(0, count)
    def _(n):
        fetch(n).wait()
        put(n).start()

    @pl.loop(0, count)
    def _(n):
        put(n).wait()


def on_device(a_panels, b_panels, a_rows, a_inner, b_inner, b_cols, c_rows, c_cols):
    partial, last = gather(a_panels, b_panels, (a_rows, a_inner, b_inner, b_cols, c_rows, c_cols))
    slots, width = c_rows.shape[2], a_panels.shape[3]
    anywhere = pl.BlockSpec(memory_space=pl.ANY)
    return pl.pallas_call(
        place_kernel,
        out_shape=jax.ShapeDtypeStruct((1, 1, slots, width, width), a_panels.dtype),
        grid_spec=pltpu.PrefetchScalarGridSpec(
            num_scalar_prefetch=1,
            grid=(),
            in_specs=[anywhere],
            out_specs=anywhere,
            scratch_shapes=[
                pltpu.VMEM((slots, width, width), a_panels.dtype),
                pltpu.SemaphoreType.DMA((slots,)),
                pltpu.SemaphoreType.DMA((slots,)),
            ],
        ),
        name="place",
    )(last, partial)


def solution(mesh):
    in_specs = (
        P("row", "col", None, None, None),
        P("row", "col", None, None, None),
        P(),
        P(),
        P(),
        P(),
        P(),
        P(),
    )
    out_specs = P("row", "col", None, None, None)
    return jax.shard_map(
        on_device, mesh=mesh, in_specs=in_specs, out_specs=out_specs, check_vma=False
    )
```

```python
import jax
import jax.numpy as jnp
import numpy as np
from jax import lax
from jax.experimental import pallas as pl
from jax.experimental.pallas import tpu as pltpu
from jax.sharding import PartitionSpec as P

STEPS = 4
MESH = pl.DeviceIdType.MESH

BLOCKS = 16
PLUS = 3
MAIN = BLOCKS - PLUS
MAIN_CHUNKS = [(at, min(2, MAIN - at)) for at in range(0, MAIN, 2)]
PLUS_CHUNKS = [(at, 1) for at in range(MAIN, BLOCKS)]
LEFT_CHUNKS = MAIN_CHUNKS + PLUS_CHUNKS
RIGHT_CHUNKS = [(at, 2) for at in range(0, BLOCKS, 2)]
N_MAIN, N_PLUS = len(MAIN_CHUNKS), len(PLUS_CHUNKS)
N_LEFT, N_RIGHT = len(LEFT_CHUNKS), len(RIGHT_CHUNKS)


def place():
    row_id, col_id = lax.axis_index("row"), lax.axis_index("col")
    return row_id // 8, (row_id // 2) % 4, row_id % 2, col_id // 2, col_id % 2


def device(x_lo, y, core, z, x_hi):
    return (x_lo * 8 + y * 2 + core, z * 2 + x_hi)


LEAD = 2
CROSS_AT = (-1, -1, -1, 1)
HALF = N_RIGHT // 2
RUN = 2
RUNS = BLOCKS // RUN
GROUP = 2 * RUN
PRODUCTS = 2 * STEPS * BLOCKS
NONE = PRODUCTS
PIECES = ((0, 0, RUNS), (1, 0, 6), (2, 0, 6), (3, 3, 1), (2, 7, 1), (3, 0, 2), (3, 4, 1), (3, 2, 1), (3, 5, 1), (1, 6, 1), (2, 6, 1), (1, 7, 1), (3, 7, 1), (3, 6, 1))
ORDERS = (
(
    ("rl", 0), ("rl", 4), ("j2", 0), ("j1", 0), ("rl", 1), ("q3", 0), ("j2", 1), ("rl", 5), ("rl", 6), ("j1", 1),
    ("j2", 2), ("q3", 1), ("j2", 3), ("rl", 2), ("q3", 2), ("rl", 3), ("j2", 4), ("j1", 2), ("rl", 7), ("i2", 0),
    ("i3", 0), ("i1", 0), ("j2", 5), ("j2", 6), ("i2", 1), ("i3", 1), ("i1", 1), ("j3", 0), ("q6", 0), ("i2", 5),
    ("j1", 3), ("i2", 2), ("q6", 1), ("i2", 6), ("i3", 5), ("i1", 5), ("j3", 1), ("i2", 4), ("j1", 4), ("i3", 2),
    ("i1", 2), ("i3", 4), ("i1", 4), ("i3", 6), ("i1", 6), ("j2", 7), ("i2", 7), ("j1", 5), ("i2", 3), ("i3", 3),
    ("i1", 3), ("q6", 2), ("j2", 8), ("i3", 7), ("i1", 7), ("j1", 6), ("j2", 9), ("j3", 4), ("j3", 2), ("j3", 3),
    ("j1", 7), ("j3", 7), ("j3", 5), ("j1", 9), ("j1", 8), ("j3", 9), ("j3", 8), ("j3", 6),
),
)


EARLY = sum(count for _, _, count in PIECES[:2]) * GROUP


def order_table():
    rank = np.zeros(PRODUCTS, np.int32)
    at = 0
    for step, first, count in PIECES:
        for block in range(first * RUN, (first + count) * RUN):
            for t in range(2):
                rank[step * 2 * BLOCKS + t * BLOCKS + block] = at
                at += 1
    return rank


def fill_tables(rows_ref, inner_ref, b_inner_ref, cols_ref, c_rows_ref, c_cols_ref, rank_row, rank_col, table, last):
    row, col = lax.axis_index("row"), lax.axis_index("col")
    i32 = jnp.int32
    down16 = lax.broadcasted_iota(i32, (BLOCKS, BLOCKS), 0)
    along16 = lax.broadcasted_iota(i32, (BLOCKS, BLOCKS), 1)

    def upright(values):
        spread = jnp.broadcast_to(values, (BLOCKS, BLOCKS))
        return jnp.sum(jnp.where(down16 == along16, spread, 0), axis=1, keepdims=True)

    picks, keys = [], []
    for step in range(STEPS):
        left_col, right_row = (col + step) % 16, (row + step) % 16
        inner = upright(inner_ref[row, pl.ds(left_col, 1), :])
        rows = upright(rows_ref[row, pl.ds(left_col, 1), :])
        b_inner = jnp.broadcast_to(b_inner_ref[right_row, pl.ds(col, 1), :], (BLOCKS, BLOCKS))
        b_cols = jnp.broadcast_to(cols_ref[right_row, pl.ds(col, 1), :], (BLOCKS, BLOCKS))
        match = inner == b_inner
        first = jnp.min(jnp.where(match, along16, BLOCKS), axis=1, keepdims=True)
        second = jnp.min(jnp.where(match & (along16 > first), along16, BLOCKS), axis=1, keepdims=True)
        for pick in (first, second):
            cols = jnp.sum(jnp.where(along16 == pick, b_cols, 0), axis=1, keepdims=True)
            picks.append(jnp.minimum(pick, BLOCKS - 1))
            keys.append(rows * 32 + cols)
    pick_col, key_col = jnp.concatenate(picks, axis=0), jnp.concatenate(keys, axis=0)
    square = (PRODUCTS, PRODUCTS)
    eye = lax.broadcasted_iota(i32, square, 0) == lax.broadcasted_iota(i32, square, 1)

    def level(values):
        return jnp.sum(jnp.where(eye, jnp.broadcast_to(values, square), 0), axis=0, keepdims=True)

    key_row = level(key_col)
    ranks = jnp.broadcast_to(rank_col[...], square)
    earlier = (jnp.broadcast_to(key_col, square) == key_row) & (ranks < rank_row[...])
    before = jnp.max(jnp.where(earlier, ranks, -1), axis=0, keepdims=True)
    table[0:1, :] = level(pick_col)
    table[1:2, :] = jnp.where(before < 0, NONE, before)
    slots = c_rows_ref.shape[2]
    slot_key = c_rows_ref[row, pl.ds(col, 1), :] * 32 + c_cols_ref[row, pl.ds(col, 1), :]
    tall = (PRODUCTS, slots)
    landed = jnp.broadcast_to(key_col, tall) == slot_key
    final = jnp.max(jnp.where(landed, jnp.broadcast_to(rank_col[...], tall), -1), axis=0, keepdims=True)
    last[...] = jnp.where(final < 0, NONE, final)


def gather_kernel(a_ref, b_ref, rows_ref, inner_ref, b_inner_ref, cols_ref, c_rows_ref, c_cols_ref, rank_row, rank_col,
                  partial, recent, last,
                  a_own, b_own, j1, j2, j3, i1, i2, i3, q3, q6, relay, sums, stage, table, plain,
                  own_sem, table_sem, stage_sem,
                  s_j1, s_j2, s_j3, s_i1, s_i2, s_i2b, s_i3, s_q3, s_q6, s_rl, s_fw, s_x,
                  r_j1, r_j2, r_j3, r_i1, r_i2, r_i3, r_q3, r_q6, r_rl):
    x_lo, y, core, z, x_hi = place()
    own = a_ref.at[0, 0]
    own_b = b_ref.at[0, 0]
    even = y % 2 == 0
    wraps1 = (3 - y) // 3
    wraps2 = 1 - y // 2
    down = device(x_lo, y, core, (z + 7) % 8, x_hi)
    up = device(x_lo, y, core, (z + 1) % 8, x_hi)
    up3 = device(x_lo, y, core, (z + 3) % 8, x_hi)
    down3 = device(x_lo, y, core, (z + 5) % 8, x_hi)
    across = device(x_lo, y, core, z, 1 - x_hi)
    twin = device(x_lo, y, 1 - core, z, x_hi)
    prev1 = device((x_lo + wraps1) % 2, (y + 3) % 4, core, z, x_hi)
    after1 = device((x_lo + y // 3) % 2, (y + 1) % 4, core, z, x_hi)
    prev2 = device((x_lo + wraps2) % 2, (y + 2) % 4, 1 - core, z, x_hi)
    after2 = device((x_lo + y // 2) % 2, (y + 2) % 4, 1 - core, z, x_hi)
    wrap = device(x_lo, (y + 3) % 4, core, z, x_hi)
    next_y = device(x_lo, (y + 1) % 4, core, z, x_hi)
    beside = device(1 - x_lo, y, core, z, x_hi)

    barrier = pltpu.get_barrier_semaphore()
    apart = device(x_lo, (y + 2) % 4, 1 - core, z, x_hi)
    beside_twin = device(1 - x_lo, y, 1 - core, z, x_hi)
    wrap_twin = device(x_lo, (y + 3) % 4, 1 - core, z, x_hi)
    next_twin = device(x_lo, (y + 1) % 4, 1 - core, z, x_hi)
    prev2_same = device((x_lo + wraps2) % 2, (y + 2) % 4, core, z, x_hi)
    after2_same = device((x_lo + y // 2) % 2, (y + 2) % 4, core, z, x_hi)
    others = (
        down, up, up3, down3, across, twin, prev1, after1, prev2, after2, wrap, next_y, beside,
        apart, beside_twin, wrap_twin, next_twin, prev2_same, after2_same,
    )
    for other in others:
        pl.semaphore_signal(barrier, inc=1, device_id=other, device_id_type=MESH)
    pl.semaphore_wait(barrier, len(others))

    take_own = [
        pltpu.make_async_copy(own, a_own, own_sem.at[0]),
        pltpu.make_async_copy(own_b, b_own, own_sem.at[1]),
    ]

    def part(ref, chunk, shift=0):
        return ref.at[pl.ds(chunk[0] - shift, chunk[1])]

    def send(src, dst, s_sem, r_sem, to):
        return pltpu.make_async_remote_copy(
            src_ref=src, dst_ref=dst, send_sem=s_sem, recv_sem=r_sem, device_id=to, device_id_type=MESH
        )

    def to_j2(k, src, to):
        return send(src, part(j2, LEFT_CHUNKS[k]), s_j2.at[k], r_j2.at[k], to)

    def to_j1(k, src):
        return send(part(src, LEFT_CHUNKS[k]), part(j1, LEFT_CHUNKS[k]), s_j1.at[k], r_j1.at[k], across)

    def to_j3(k, src, to):
        return send(src, part(j3, LEFT_CHUNKS[k]), s_j3.at[k], r_j3.at[k], to)

    def to_q3(k):
        chunk = PLUS_CHUNKS[k]
        return send(part(own, chunk), part(q3, chunk, MAIN), s_q3.at[k], r_q3.at[k], up3)

    def to_q6(k):
        chunk = PLUS_CHUNKS[k]
        return send(part(q3, chunk, MAIN), part(q6, chunk, MAIN), s_q6.at[k], r_q6.at[k], up3)

    def to_right(k, src, dst, s_sem, r_sem, to):
        return send(part(src, RIGHT_CHUNKS[k]), part(dst, RIGHT_CHUNKS[k]), s_sem.at[k], r_sem.at[k], to)

    def cross(k):
        @pl.when((core == 0) & (y == 0))
        def _():
            to_right(k, own_b, i3, s_i3, r_i3, prev2).start()

        @pl.when((core == 0) & (y == 1))
        def _():
            to_right(k, own_b, relay, s_rl, r_rl, beside).start()

    for k in range(N_PLUS):
        to_q3(k).start()
    for k in range(max(N_MAIN, N_RIGHT)):
        if k < N_MAIN:
            to_j2(k, part(own, LEFT_CHUNKS[k]), down).start()
        if k < LEAD:

            @pl.when(x_hi == 1)
            def _():
                to_j1(k, own).start()

        if k < N_RIGHT:

            @pl.when(core == 0)
            def _():
                @pl.when(y % 2 == 1)
                def _():
                    to_right(k, own_b, i2, s_i2b, r_i2, prev1).start()

                @pl.when(y == 2)
                def _():
                    to_right(k, own_b, i3, s_i3, r_i3, prev2).start()

                if k >= HALF:

                    @pl.when(y < 2)
                    def _():
                        to_right(k, own_b, relay, s_rl, r_rl, twin).start()

            @pl.when(core == 1)
            def _():
                to_right(k, own_b, i1, s_i1, r_i1, twin).start()

                @pl.when(y == 0)
                def _():
                    to_right(k, own_b, relay, s_rl, r_rl, wrap if k < HALF else wrap_twin).start()

                @pl.when(y != 0)
                def _():
                    to_right(k, own_b, i2, s_i2, r_i2, prev1).start()

    @pl.when((core == 0) & (y == 3))
    def _():
        for k in range(N_RIGHT):
            to_right(k, own_b, i3, s_i3, r_i3, prev2).start()

    for k in range(HALF):
        if CROSS_AT[k] < 0:
            cross(k)

    for copy in take_own:
        copy.start()
    fill_tables(rows_ref, inner_ref, b_inner_ref, cols_ref, c_rows_ref, c_cols_ref, rank_row, rank_col, table, last)
    to_plain = pltpu.make_async_copy(table, plain, table_sem)
    to_plain.start()
    sums[NONE] = jnp.zeros(sums.shape[1:], sums.dtype)
    stage[...] = jnp.zeros(stage.shape, stage.dtype)

    def put(group):
        return pltpu.make_async_copy(
            stage.at[group % 2], partial.at[pl.ds(group * GROUP, GROUP)], stage_sem.at[group % 2]
        )

    for n in range(2):
        put(EARLY // GROUP + n).start()
    recent[PRODUCTS - EARLY] = jnp.zeros(recent.shape[1:], recent.dtype)
    to_plain.wait()

    def on_j2(k):
        to_j2(k, part(own, LEFT_CHUNKS[k]), down).wait_recv()

        @pl.when(x_hi == 0)
        def _():
            to_j1(k, j2).start()

        if k + LEAD < N_LEFT:

            @pl.when(x_hi == 1)
            def _():
                to_j1(k + LEAD, own).start()

        if k >= N_MAIN:

            @pl.when(x_hi == 1)
            def _():
                to_j3(k, part(j2, LEFT_CHUNKS[k]), across).start()

        for n in range(HALF):
            if CROSS_AT[n] == k:
                cross(n)

    def on_j1(k):
        to_j1(k, own).wait_recv()
        if k < N_MAIN:
            to_j3(k, part(j1, LEFT_CHUNKS[k]), down).start()

    def on_j3(k):
        to_j3(k, part(j1, LEFT_CHUNKS[k]), down).wait_recv()

    def on_q3(k):
        to_q3(k).wait_recv()
        to_q6(k).start()

    def on_q6(k):
        to_q6(k).wait_recv()
        mine = part(q6, PLUS_CHUNKS[k], MAIN)
        to_j2(N_MAIN + k, mine, up).start()

        @pl.when(x_hi == 0)
        def _():
            to_j3(N_MAIN + k, mine, across).start()

    def on_i1(k):
        to_right(k, own_b, i1, s_i1, r_i1, twin).wait_recv()

        @pl.when((core == 1) & (y % 2 == 1))
        def _():
            to_right(k, i1, i2, s_i2b, r_i2, twin).start()

    def on_i2(k):
        to_right(k, own_b, i2, s_i2, r_i2, prev1).wait_recv()

        @pl.when(core == 1)
        def _():
            to_right(k, i2, i3, s_i3, r_i3, twin).start()

        @pl.when((core == 0) & (y % 2 == 0))
        def _():
            to_right(k, i2, i1, s_i1, r_i1, twin).start()

    def on_i3(k):
        to_right(k, own_b, i3, s_i3, r_i3, prev2).wait_recv()

        @pl.when((core == 1) & (y % 2 == 0))
        def _():
            to_right(k, i3, i1, s_fw, r_i1, next_y).start()

    def on_relay(k):
        arrived = to_right(k, own_b, relay, s_rl, r_rl, wrap)
        if k >= HALF:

            @pl.when((core == 1) & (y == 0))
            def _():
                arrived.wait_recv()
                to_right(k, relay, i3, s_x, r_i3, prev2_same).start()

            @pl.when((core == 1) & (y == 1))
            def _():
                arrived.wait_recv()
                to_right(k, relay, relay, s_x, r_rl, beside_twin).start()

        @pl.when((core == 0) & (y == 1))
        def _():
            arrived.wait_recv()
            to_right(k, relay, i3, s_i3, r_i3, apart).start()

        @pl.when((core == (1 if k < HALF else 0)) & (y == 3))
        def _():
            arrived.wait_recv()
            to_right(k, relay, i2, s_x, r_i2, beside if k < HALF else beside_twin).start()

    lefts, rights = (a_own, j1, j2, j3), (b_own, i1, i2, i3)

    def multiply_run(step, run, group, early):
        if early:
            put(group).wait()
        for n in range(RUN):
            block = lefts[step][run * RUN + n]
            for t in range(2):
                j = step * 2 * BLOCKS + t * BLOCKS + run * RUN + n
                rank = group * GROUP + 2 * n + t
                total = sums[plain[1, j]] + jnp.dot(
                    block, rights[step][plain[0, j]], preferred_element_type=jnp.float32
                )
                sums[rank] = total
                if early:
                    stage[group % 2, 2 * n + t] = total.astype(stage.dtype)
                else:
                    recent[rank - EARLY] = total.astype(recent.dtype)
        if early:
            put(group).start()

    def multiply(step, first, count, group):
        early = group * GROUP < EARLY
        if count == 1:
            multiply_run(step, first, group, early)
        else:

            @pl.loop(0, count)
            def _(n):
                multiply_run(step, first + n, group + n, early)

    handlers = {
        "j1": on_j1, "j2": on_j2, "j3": on_j3, "q3": on_q3, "q6": on_q6,
        "i1": on_i1, "i2": on_i2, "i3": on_i3, "rl": on_relay,
    }

    for copy in take_own:
        copy.wait()
    multiply(*PIECES[0], 0)

    def follow(order):
        for event in with_products(order):
            if event[0] == "x":
                multiply(*event[1:])
            else:
                handlers[event[0]](event[1])

    if len(ORDERS) == 1:
        follow(ORDERS[0])
    else:
        for which, order in enumerate(ORDERS):

            @pl.when(core == which)
            def _():
                follow(order)

    for group in range(2):
        put(group).wait()

    for k in range(N_LEFT):
        chunk = LEFT_CHUNKS[k]
        to_j2(k, part(own, chunk), down).wait_send()
        to_j1(k, own).wait_send()
        to_j3(k, part(own, chunk), down).wait_send()
    for k in range(N_PLUS):
        to_q3(k).wait_send()
        to_q6(k).wait_send()
    for k in range(N_RIGHT):
        first_half = k < HALF

        @pl.when((core == 1) | (y != 0) | first_half)
        def _():
            to_right(k, own_b, i3, s_i3, r_i3, twin).wait_send()

        @pl.when((core == 1) | even)
        def _():
            to_right(k, own_b, i1, s_i1, r_i1, twin).wait_send()

        @pl.when(y % 2 == 1)
        def _():
            to_right(k, own_b, i2, s_i2b, r_i2, twin).wait_send()

        @pl.when((core == 1) & (y != 0))
        def _():
            to_right(k, own_b, i2, s_i2, r_i2, prev1).wait_send()

        @pl.when((core == 1) & even)
        def _():
            to_right(k, own_b, i1, s_fw, r_i1, next_y).wait_send()

        if first_half:
            staged, passed = ((core == 0) & (y == 1)) | ((core == 1) & (y == 0)), (core == 1) & (y == 3)
        else:
            staged = ((core == 0) & (y < 2)) | ((core == 1) & (y == 0))
            passed = ((core == 1) & (y < 2)) | ((core == 0) & (y == 3))

        @pl.when(staged)
        def _():
            to_right(k, own_b, relay, s_rl, r_rl, wrap).wait_send()

        @pl.when(passed)
        def _():
            to_right(k, own_b, relay, s_x, r_rl, wrap).wait_send()


def with_products(order):
    todo, group = [], RUNS
    for step, first, count in PIECES[1:]:
        blocks = set(range(first * RUN, (first + count) * RUN))
        chunks = {k for k, (at, n) in enumerate(LEFT_CHUNKS) if blocks & set(range(at, at + n))}
        needs = {(f"j{step}", k) for k in chunks} | {(f"i{step}", k) for k in range(N_RIGHT)}
        todo.append((needs, ("x", step, first, count, group)))
        group += count
    done, out = set(), []
    for event in order:
        out.append(event)
        done.add(event)
        while todo and todo[0][0] <= done:
            out.append(todo.pop(0)[1])
    return out


def gather(a_panels, b_panels, indices):
    dtype = a_panels.dtype
    tail = a_panels.shape[3:]
    slots = indices[-1].shape[2]
    rank = order_table()
    anywhere = pl.BlockSpec(memory_space=pl.ANY)
    in_vmem = pl.BlockSpec(memory_space=pltpu.VMEM)
    sems = [2, 1, 2]
    sems += [N_LEFT] * 3 + [N_RIGHT] * 4 + [N_PLUS] * 2 + [N_RIGHT] * 3
    sems += [N_LEFT] * 3 + [N_RIGHT] * 3 + [N_PLUS] * 2 + [N_RIGHT]
    scratch = [pltpu.VMEM((BLOCKS, *tail), dtype)] * 8 + [pltpu.VMEM((PLUS, *tail), dtype)] * 2
    scratch += [
        pltpu.VMEM((BLOCKS, *tail), dtype),
        pltpu.VMEM((PRODUCTS + 1, *tail), jnp.float32),
        pltpu.VMEM((2, GROUP, *tail), dtype),
        pltpu.VMEM((8, PRODUCTS), jnp.int32),
        pltpu.SMEM((8, PRODUCTS), jnp.int32),
    ]
    return pl.pallas_call(
        gather_kernel,
        out_shape=[
            jax.ShapeDtypeStruct((EARLY + 2 * GROUP + PRODUCTS, *tail), dtype),
            pltpu.VMEM((PRODUCTS - EARLY + 1, *tail), dtype),
            jax.ShapeDtypeStruct((1, slots), jnp.int32),
        ],
        in_specs=[anywhere] * 2 + [in_vmem] * 8,
        out_specs=[pl.BlockSpec(memory_space=pltpu.HBM), in_vmem, in_vmem],
        scratch_shapes=scratch + [pltpu.SemaphoreType.DMA((n,)) if n > 1 else pltpu.SemaphoreType.DMA for n in sems],
        compiler_params=pltpu.CompilerParams(collective_id=0, has_side_effects=True, vmem_limit_bytes=57000000),
        name="gather",
    )(a_panels, b_panels, *indices, jnp.asarray(rank)[None, :], jnp.asarray(rank)[:, None])


def place_kernel(last, partial, recent, out, stage, in_sem, out_sem):
    count = stage.shape[0]

    def fetch(n, rank):
        return pltpu.make_async_copy(partial.at[rank], stage.at[n], in_sem.at[n])

    def put(n, src):
        return pltpu.make_async_copy(src, out.at[0, 0, n], out_sem.at[n])

    @pl.loop(0, count)
    def _(n):
        rank = last[0, n]

        @pl.when(rank < EARLY)
        def _():
            fetch(n, rank).start()

        @pl.when(rank >= EARLY)
        def _():
            put(n, recent.at[rank - EARLY]).start()

    @pl.loop(0, count)
    def _(n):
        rank = last[0, n]

        @pl.when(rank < EARLY)
        def _():
            fetch(n, rank).wait()
            put(n, stage.at[n]).start()

    @pl.loop(0, count)
    def _(n):
        put(n, stage.at[n]).wait()


def on_device(a_panels, b_panels, a_rows, a_inner, b_inner, b_cols, c_rows, c_cols):
    partial, recent, last = gather(a_panels, b_panels, (a_rows, a_inner, b_inner, b_cols, c_rows, c_cols))
    slots, width = c_rows.shape[2], a_panels.shape[3]
    anywhere = pl.BlockSpec(memory_space=pl.ANY)
    return pl.pallas_call(
        place_kernel,
        out_shape=jax.ShapeDtypeStruct((1, 1, slots, width, width), a_panels.dtype),
        grid_spec=pltpu.PrefetchScalarGridSpec(
            num_scalar_prefetch=1,
            grid=(),
            in_specs=[pl.BlockSpec(memory_space=pltpu.HBM), anywhere],
            out_specs=anywhere,
            scratch_shapes=[
                pltpu.VMEM((slots, width, width), a_panels.dtype),
                pltpu.SemaphoreType.DMA((slots,)),
                pltpu.SemaphoreType.DMA((slots,)),
            ],
        ),
        compiler_params=pltpu.CompilerParams(vmem_limit_bytes=38000000),
        name="place",
    )(last, partial, recent)


def solution(mesh):
    in_specs = (
        P("row", "col", None, None, None),
        P("row", "col", None, None, None),
        P(),
        P(),
        P(),
        P(),
        P(),
        P(),
    )
    out_specs = P("row", "col", None, None, None)
    return jax.shard_map(
        on_device, mesh=mesh, in_specs=in_specs, out_specs=out_specs, check_vma=False
    )
```

```python
import jax
import jax.numpy as jnp
import numpy as np
from jax import lax
from jax.experimental import pallas as pl
from jax.experimental.pallas import tpu as pltpu
from jax.sharding import PartitionSpec as P

STEPS = 4
MESH = pl.DeviceIdType.MESH

BLOCKS = 16
PLUS = 3
MAIN = BLOCKS - PLUS
MAIN_CHUNKS = [(at, min(2, MAIN - at)) for at in range(0, MAIN, 2)]
PLUS_CHUNKS = [(at, 1) for at in range(MAIN, BLOCKS)]
LEFT_CHUNKS = MAIN_CHUNKS + PLUS_CHUNKS
RIGHT_CHUNKS = [(at, 2) for at in range(0, BLOCKS, 2)]
N_MAIN, N_PLUS = len(MAIN_CHUNKS), len(PLUS_CHUNKS)
N_LEFT, N_RIGHT = len(LEFT_CHUNKS), len(RIGHT_CHUNKS)


def place():
    row_id, col_id = lax.axis_index("row"), lax.axis_index("col")
    return row_id // 8, (row_id // 2) % 4, row_id % 2, col_id // 2, col_id % 2


def device(x_lo, y, core, z, x_hi):
    return (x_lo * 8 + y * 2 + core, z * 2 + x_hi)


LEAD = 2
CROSS_AT = (-1, -1, -1, 1)
HALF = N_RIGHT // 2
RUN = 2
RUNS = BLOCKS // RUN
GROUP = 2 * RUN
PRODUCTS = 2 * STEPS * BLOCKS
NONE = PRODUCTS
PIECES = ((0, 0, RUNS), (1, 0, 6), (2, 0, 6), (3, 3, 1), (2, 7, 1), (3, 0, 2), (3, 4, 1), (3, 2, 1), (3, 5, 1), (1, 6, 1), (2, 6, 1), (1, 7, 1), (3, 7, 1), (3, 6, 1))
ORDERS = (
(
    ("rl", 0), ("rl", 4), ("j2", 0), ("j1", 0), ("rl", 1), ("q3", 0), ("j2", 1), ("rl", 5), ("rl", 6), ("j1", 1),
    ("j2", 2), ("q3", 1), ("j2", 3), ("rl", 2), ("q3", 2), ("rl", 3), ("j2", 4), ("j1", 2), ("rl", 7), ("i2", 0),
    ("i3", 0), ("i1", 0), ("j2", 5), ("j2", 6), ("i2", 1), ("i3", 1), ("i1", 1), ("j3", 0), ("q6", 0), ("i2", 5),
    ("j1", 3), ("i2", 2), ("q6", 1), ("i2", 6), ("i3", 5), ("i1", 5), ("j3", 1), ("i2", 4), ("j1", 4), ("i3", 2),
    ("i1", 2), ("i3", 4), ("i1", 4), ("i3", 6), ("i1", 6), ("j2", 7), ("i2", 7), ("j1", 5), ("i2", 3), ("i3", 3),
    ("i1", 3), ("q6", 2), ("j2", 8), ("i3", 7), ("i1", 7), ("j1", 6), ("j2", 9), ("j3", 4), ("j3", 2), ("j3", 3),
    ("j1", 7), ("j3", 7), ("j3", 5), ("j1", 9), ("j1", 8), ("j3", 9), ("j3", 8), ("j3", 6),
),
)


EARLY = sum(count for _, _, count in PIECES[:2]) * GROUP


def order_table():
    rank = np.zeros(PRODUCTS, np.int32)
    at = 0
    for step, first, count in PIECES:
        for block in range(first * RUN, (first + count) * RUN):
            for t in range(2):
                rank[step * 2 * BLOCKS + t * BLOCKS + block] = at
                at += 1
    return rank


def fill_tables(rows_ref, inner_ref, b_inner_ref, cols_ref, c_rows_ref, c_cols_ref, rank_row, rank_col, table, last):
    row, col = lax.axis_index("row"), lax.axis_index("col")
    i32 = jnp.int32
    down16 = lax.broadcasted_iota(i32, (BLOCKS, BLOCKS), 0)
    along16 = lax.broadcasted_iota(i32, (BLOCKS, BLOCKS), 1)

    def upright(values):
        spread = jnp.broadcast_to(values, (BLOCKS, BLOCKS))
        return jnp.sum(jnp.where(down16 == along16, spread, 0), axis=1, keepdims=True)

    picks, keys = [], []
    for step in range(STEPS):
        left_col, right_row = (col + step) % 16, (row + step) % 16
        inner = upright(inner_ref[row, pl.ds(left_col, 1), :])
        rows = upright(rows_ref[row, pl.ds(left_col, 1), :])
        b_inner = jnp.broadcast_to(b_inner_ref[right_row, pl.ds(col, 1), :], (BLOCKS, BLOCKS))
        b_cols = jnp.broadcast_to(cols_ref[right_row, pl.ds(col, 1), :], (BLOCKS, BLOCKS))
        match = inner == b_inner
        first = jnp.min(jnp.where(match, along16, BLOCKS), axis=1, keepdims=True)
        second = jnp.min(jnp.where(match & (along16 > first), along16, BLOCKS), axis=1, keepdims=True)
        for pick in (first, second):
            cols = jnp.sum(jnp.where(along16 == pick, b_cols, 0), axis=1, keepdims=True)
            picks.append(jnp.minimum(pick, BLOCKS - 1))
            keys.append(rows * 32 + cols)
    pick_col, key_col = jnp.concatenate(picks, axis=0), jnp.concatenate(keys, axis=0)
    square = (PRODUCTS, PRODUCTS)
    eye = lax.broadcasted_iota(i32, square, 0) == lax.broadcasted_iota(i32, square, 1)

    def level(values):
        return jnp.sum(jnp.where(eye, jnp.broadcast_to(values, square), 0), axis=0, keepdims=True)

    key_row = level(key_col)
    ranks = jnp.broadcast_to(rank_col[...], square)
    earlier = (jnp.broadcast_to(key_col, square) == key_row) & (ranks < rank_row[...])
    before = jnp.max(jnp.where(earlier, ranks, -1), axis=0, keepdims=True)
    table[0:1, :] = level(pick_col)
    table[1:2, :] = jnp.where(before < 0, NONE, before)
    slots = c_rows_ref.shape[2]
    slot_key = c_rows_ref[row, pl.ds(col, 1), :] * 32 + c_cols_ref[row, pl.ds(col, 1), :]
    tall = (PRODUCTS, slots)
    landed = jnp.broadcast_to(key_col, tall) == slot_key
    final = jnp.max(jnp.where(landed, jnp.broadcast_to(rank_col[...], tall), -1), axis=0, keepdims=True)
    last[...] = jnp.where(final < 0, NONE, final)


def gather_kernel(a_ref, b_ref, rows_ref, inner_ref, b_inner_ref, cols_ref, c_rows_ref, c_cols_ref, rank_row, rank_col,
                  partial, recent, last,
                  a_own, b_own, j1, j2, j3, i1, i2, i3, q3, q6, relay, sums, stage, table, plain,
                  own_sem, table_sem, stage_sem,
                  s_j1, s_j2, s_j3, s_i1, s_i2, s_i2b, s_i3, s_q3, s_q6, s_rl, s_fw, s_x,
                  r_j1, r_j2, r_j3, r_i1, r_i2, r_i3, r_q3, r_q6, r_rl):
    x_lo, y, core, z, x_hi = place()
    own = a_ref.at[0, 0]
    own_b = b_ref.at[0, 0]
    even = y % 2 == 0
    wraps1 = (3 - y) // 3
    wraps2 = 1 - y // 2
    down = device(x_lo, y, core, (z + 7) % 8, x_hi)
    up = device(x_lo, y, core, (z + 1) % 8, x_hi)
    up3 = device(x_lo, y, core, (z + 3) % 8, x_hi)
    down3 = device(x_lo, y, core, (z + 5) % 8, x_hi)
    across = device(x_lo, y, core, z, 1 - x_hi)
    twin = device(x_lo, y, 1 - core, z, x_hi)
    prev1 = device((x_lo + wraps1) % 2, (y + 3) % 4, core, z, x_hi)
    after1 = device((x_lo + y // 3) % 2, (y + 1) % 4, core, z, x_hi)
    prev2 = device((x_lo + wraps2) % 2, (y + 2) % 4, 1 - core, z, x_hi)
    after2 = device((x_lo + y // 2) % 2, (y + 2) % 4, 1 - core, z, x_hi)
    wrap = device(x_lo, (y + 3) % 4, core, z, x_hi)
    next_y = device(x_lo, (y + 1) % 4, core, z, x_hi)
    beside = device(1 - x_lo, y, core, z, x_hi)

    barrier = pltpu.get_barrier_semaphore()
    apart = device(x_lo, (y + 2) % 4, 1 - core, z, x_hi)
    beside_twin = device(1 - x_lo, y, 1 - core, z, x_hi)
    wrap_twin = device(x_lo, (y + 3) % 4, 1 - core, z, x_hi)
    next_twin = device(x_lo, (y + 1) % 4, 1 - core, z, x_hi)
    prev2_same = device((x_lo + wraps2) % 2, (y + 2) % 4, core, z, x_hi)
    after2_same = device((x_lo + y // 2) % 2, (y + 2) % 4, core, z, x_hi)
    others = (
        down, up, up3, down3, across, twin, prev1, after1, prev2, after2, wrap, next_y, beside,
        apart, beside_twin, wrap_twin, next_twin, prev2_same, after2_same,
    )
    for other in others:
        pl.semaphore_signal(barrier, inc=1, device_id=other, device_id_type=MESH)
    pl.semaphore_wait(barrier, len(others))

    take_own = [
        pltpu.make_async_copy(own, a_own, own_sem.at[0]),
        pltpu.make_async_copy(own_b, b_own, own_sem.at[1]),
    ]

    def part(ref, chunk, shift=0):
        return ref.at[pl.ds(chunk[0] - shift, chunk[1])]

    def send(src, dst, s_sem, r_sem, to):
        return pltpu.make_async_remote_copy(
            src_ref=src, dst_ref=dst, send_sem=s_sem, recv_sem=r_sem, device_id=to, device_id_type=MESH
        )

    def to_j2(k, src, to):
        return send(src, part(j2, LEFT_CHUNKS[k]), s_j2.at[k], r_j2.at[k], to)

    def to_j1(k, src):
        return send(part(src, LEFT_CHUNKS[k]), part(j1, LEFT_CHUNKS[k]), s_j1.at[k], r_j1.at[k], across)

    def to_j3(k, src, to):
        return send(src, part(j3, LEFT_CHUNKS[k]), s_j3.at[k], r_j3.at[k], to)

    def to_q3(k):
        chunk = PLUS_CHUNKS[k]
        return send(part(own, chunk), part(q3, chunk, MAIN), s_q3.at[k], r_q3.at[k], up3)

    def to_q6(k):
        chunk = PLUS_CHUNKS[k]
        return send(part(q3, chunk, MAIN), part(q6, chunk, MAIN), s_q6.at[k], r_q6.at[k], up3)

    def to_right(k, src, dst, s_sem, r_sem, to):
        return send(part(src, RIGHT_CHUNKS[k]), part(dst, RIGHT_CHUNKS[k]), s_sem.at[k], r_sem.at[k], to)

    def cross(k):
        @pl.when((core == 0) & (y == 0))
        def _():
            to_right(k, own_b, i3, s_i3, r_i3, prev2).start()

        @pl.when((core == 0) & (y == 1))
        def _():
            to_right(k, own_b, relay, s_rl, r_rl, beside).start()

    for k in range(N_PLUS):
        to_q3(k).start()
    for k in range(max(N_MAIN, N_RIGHT)):
        if k < N_MAIN:
            to_j2(k, part(own, LEFT_CHUNKS[k]), down).start()
        if k < LEAD:

            @pl.when(x_hi == 1)
            def _():
                to_j1(k, own).start()

        if k < N_RIGHT:

            @pl.when(core == 0)
            def _():
                @pl.when(y % 2 == 1)
                def _():
                    to_right(k, own_b, i2, s_i2b, r_i2, prev1).start()

                @pl.when(y == 2)
                def _():
                    to_right(k, own_b, i3, s_i3, r_i3, prev2).start()

                if k >= HALF:

                    @pl.when(y < 2)
                    def _():
                        to_right(k, own_b, relay, s_rl, r_rl, twin).start()

            @pl.when(core == 1)
            def _():
                to_right(k, own_b, i1, s_i1, r_i1, twin).start()

                @pl.when(y == 0)
                def _():
                    to_right(k, own_b, relay, s_rl, r_rl, wrap if k < HALF else wrap_twin).start()

                @pl.when(y != 0)
                def _():
                    to_right(k, own_b, i2, s_i2, r_i2, prev1).start()

    @pl.when((core == 0) & (y == 3))
    def _():
        for k in range(N_RIGHT):
            to_right(k, own_b, i3, s_i3, r_i3, prev2).start()

    for k in range(HALF):
        if CROSS_AT[k] < 0:
            cross(k)

    for copy in take_own:
        copy.start()
    fill_tables(rows_ref, inner_ref, b_inner_ref, cols_ref, c_rows_ref, c_cols_ref, rank_row, rank_col, table, last)
    to_plain = pltpu.make_async_copy(table, plain, table_sem)
    to_plain.start()
    sums[NONE] = jnp.zeros(sums.shape[1:], sums.dtype)
    stage[...] = jnp.zeros(stage.shape, stage.dtype)

    def put(group):
        return pltpu.make_async_copy(
            stage.at[group % 2], partial.at[pl.ds(group * GROUP, GROUP)], stage_sem.at[group % 2]
        )

    for n in range(2):
        put(EARLY // GROUP + n).start()
    recent[PRODUCTS - EARLY] = jnp.zeros(recent.shape[1:], recent.dtype)
    to_plain.wait()

    def on_j2(k):
        to_j2(k, part(own, LEFT_CHUNKS[k]), down).wait_recv()

        @pl.when(x_hi == 0)
        def _():
            to_j1(k, j2).start()

        if k + LEAD < N_LEFT:

            @pl.when(x_hi == 1)
            def _():
                to_j1(k + LEAD, own).start()

        if k >= N_MAIN:

            @pl.when(x_hi == 1)
            def _():
                to_j3(k, part(j2, LEFT_CHUNKS[k]), across).start()

        for n in range(HALF):
            if CROSS_AT[n] == k:
                cross(n)

    def on_j1(k):
        to_j1(k, own).wait_recv()
        if k < N_MAIN:
            to_j3(k, part(j1, LEFT_CHUNKS[k]), down).start()

    def on_j3(k):
        to_j3(k, part(j1, LEFT_CHUNKS[k]), down).wait_recv()

    def on_q3(k):
        to_q3(k).wait_recv()
        to_q6(k).start()

    def on_q6(k):
        to_q6(k).wait_recv()
        mine = part(q6, PLUS_CHUNKS[k], MAIN)
        to_j2(N_MAIN + k, mine, up).start()

        @pl.when(x_hi == 0)
        def _():
            to_j3(N_MAIN + k, mine, across).start()

    def on_i1(k):
        to_right(k, own_b, i1, s_i1, r_i1, twin).wait_recv()

        @pl.when((core == 1) & (y % 2 == 1))
        def _():
            to_right(k, i1, i2, s_i2b, r_i2, twin).start()

    def on_i2(k):
        to_right(k, own_b, i2, s_i2, r_i2, prev1).wait_recv()

        @pl.when(core == 1)
        def _():
            to_right(k, i2, i3, s_i3, r_i3, twin).start()

        @pl.when((core == 0) & (y % 2 == 0))
        def _():
            to_right(k, i2, i1, s_i1, r_i1, twin).start()

    def on_i3(k):
        to_right(k, own_b, i3, s_i3, r_i3, prev2).wait_recv()

        @pl.when((core == 1) & (y % 2 == 0))
        def _():
            to_right(k, i3, i1, s_fw, r_i1, next_y).start()

    def on_relay(k):
        arrived = to_right(k, own_b, relay, s_rl, r_rl, wrap)
        if k >= HALF:

            @pl.when((core == 1) & (y == 0))
            def _():
                arrived.wait_recv()
                to_right(k, relay, i3, s_x, r_i3, prev2_same).start()

            @pl.when((core == 1) & (y == 1))
            def _():
                arrived.wait_recv()
                to_right(k, relay, relay, s_x, r_rl, beside_twin).start()

        @pl.when((core == 0) & (y == 1))
        def _():
            arrived.wait_recv()
            to_right(k, relay, i3, s_i3, r_i3, apart).start()

        @pl.when((core == (1 if k < HALF else 0)) & (y == 3))
        def _():
            arrived.wait_recv()
            to_right(k, relay, i2, s_x, r_i2, beside if k < HALF else beside_twin).start()

    lefts, rights = (a_own, j1, j2, j3), (b_own, i1, i2, i3)

    def multiply_run(step, run, group, early):
        if early:
            put(group).wait()
        for n in range(RUN):
            block = lefts[step][run * RUN + n]
            for t in range(2):
                j = step * 2 * BLOCKS + t * BLOCKS + run * RUN + n
                rank = group * GROUP + 2 * n + t
                total = sums[plain[1, j]] + jnp.dot(
                    block, rights[step][plain[0, j]], preferred_element_type=jnp.float32
                )
                sums[rank] = total
                if early:
                    stage[group % 2, 2 * n + t] = total.astype(stage.dtype)
                else:
                    recent[rank - EARLY] = total.astype(recent.dtype)
        if early:
            put(group).start()

    def multiply(step, first, count, group):
        early = group * GROUP < EARLY
        if count == 1:
            multiply_run(step, first, group, early)
        else:

            @pl.loop(0, count)
            def _(n):
                multiply_run(step, first + n, group + n, early)

    handlers = {
        "j1": on_j1, "j2": on_j2, "j3": on_j3, "q3": on_q3, "q6": on_q6,
        "i1": on_i1, "i2": on_i2, "i3": on_i3, "rl": on_relay,
    }

    for copy in take_own:
        copy.wait()
    multiply(*PIECES[0], 0)

    def follow(order):
        for event in with_products(order):
            if event[0] == "x":
                multiply(*event[1:])
            else:
                handlers[event[0]](event[1])

    if len(ORDERS) == 1:
        follow(ORDERS[0])
    else:
        for which, order in enumerate(ORDERS):

            @pl.when(core == which)
            def _():
                follow(order)

    for group in range(2):
        put(group).wait()

    for k in range(N_LEFT):
        chunk = LEFT_CHUNKS[k]
        to_j2(k, part(own, chunk), down).wait_send()
        to_j1(k, own).wait_send()
        to_j3(k, part(own, chunk), down).wait_send()
    for k in range(N_PLUS):
        to_q3(k).wait_send()
        to_q6(k).wait_send()
    for k in range(N_RIGHT):
        first_half = k < HALF

        @pl.when((core == 1) | (y != 0) | first_half)
        def _():
            to_right(k, own_b, i3, s_i3, r_i3, twin).wait_send()

        @pl.when((core == 1) | even)
        def _():
            to_right(k, own_b, i1, s_i1, r_i1, twin).wait_send()

        @pl.when(y % 2 == 1)
        def _():
            to_right(k, own_b, i2, s_i2b, r_i2, twin).wait_send()

        @pl.when((core == 1) & (y != 0))
        def _():
            to_right(k, own_b, i2, s_i2, r_i2, prev1).wait_send()

        @pl.when((core == 1) & even)
        def _():
            to_right(k, own_b, i1, s_fw, r_i1, next_y).wait_send()

        if first_half:
            staged, passed = ((core == 0) & (y == 1)) | ((core == 1) & (y == 0)), (core == 1) & (y == 3)
        else:
            staged = ((core == 0) & (y < 2)) | ((core == 1) & (y == 0))
            passed = ((core == 1) & (y < 2)) | ((core == 0) & (y == 3))

        @pl.when(staged)
        def _():
            to_right(k, own_b, relay, s_rl, r_rl, wrap).wait_send()

        @pl.when(passed)
        def _():
            to_right(k, own_b, relay, s_x, r_rl, wrap).wait_send()


def with_products(order):
    todo, group = [], RUNS
    for step, first, count in PIECES[1:]:
        blocks = set(range(first * RUN, (first + count) * RUN))
        chunks = {k for k, (at, n) in enumerate(LEFT_CHUNKS) if blocks & set(range(at, at + n))}
        needs = {(f"j{step}", k) for k in chunks} | {(f"i{step}", k) for k in range(N_RIGHT)}
        todo.append((needs, ("x", step, first, count, group)))
        group += count
    done, out = set(), []
    for event in order:
        out.append(event)
        done.add(event)
        while todo and todo[0][0] <= done:
            out.append(todo.pop(0)[1])
    return out


def gather(a_panels, b_panels, indices):
    dtype = a_panels.dtype
    tail = a_panels.shape[3:]
    slots = indices[-1].shape[2]
    rank = order_table()
    anywhere = pl.BlockSpec(memory_space=pl.ANY)
    in_vmem = pl.BlockSpec(memory_space=pltpu.VMEM)
    sems = [2, 1, 2]
    sems += [N_LEFT] * 3 + [N_RIGHT] * 4 + [N_PLUS] * 2 + [N_RIGHT] * 3
    sems += [N_LEFT] * 3 + [N_RIGHT] * 3 + [N_PLUS] * 2 + [N_RIGHT]
    scratch = [pltpu.VMEM((BLOCKS, *tail), dtype)] * 8 + [pltpu.VMEM((PLUS, *tail), dtype)] * 2
    scratch += [
        pltpu.VMEM((BLOCKS, *tail), dtype),
        pltpu.VMEM((PRODUCTS + 1, *tail), jnp.float32),
        pltpu.VMEM((2, GROUP, *tail), dtype),
        pltpu.VMEM((8, PRODUCTS), jnp.int32),
        pltpu.SMEM((8, PRODUCTS), jnp.int32),
    ]
    return pl.pallas_call(
        gather_kernel,
        out_shape=[
            jax.ShapeDtypeStruct((EARLY + 2 * GROUP + PRODUCTS, *tail), dtype),
            pltpu.VMEM((PRODUCTS - EARLY + 1, *tail), dtype),
            jax.ShapeDtypeStruct((1, slots), jnp.int32),
        ],
        in_specs=[anywhere] * 2 + [in_vmem] * 8,
        out_specs=[pl.BlockSpec(memory_space=pltpu.HBM), in_vmem, in_vmem],
        scratch_shapes=scratch + [pltpu.SemaphoreType.DMA((n,)) if n > 1 else pltpu.SemaphoreType.DMA for n in sems],
        compiler_params=pltpu.CompilerParams(collective_id=0, has_side_effects=True, vmem_limit_bytes=57000000),
        name="gather",
    )(a_panels, b_panels, *indices, jnp.asarray(rank)[None, :], jnp.asarray(rank)[:, None])


def place_kernel(last, partial, recent, out, stage, in_sem, out_sem):
    count = stage.shape[0]

    def fetch(n, rank):
        return pltpu.make_async_copy(partial.at[rank], stage.at[n], in_sem.at[n])

    def put(n, src):
        return pltpu.make_async_copy(src, out.at[0, 0, n], out_sem.at[n])

    @pl.loop(0, count, unroll=8)
    def _(n):
        rank = last[0, n]

        @pl.when(rank < EARLY)
        def _():
            fetch(n, rank).start()

    @pl.loop(0, count, unroll=8)
    def _(n):
        rank = last[0, n]

        @pl.when(rank >= EARLY)
        def _():
            put(n, recent.at[rank - EARLY]).start()

    @pl.loop(0, count, unroll=8)
    def _(n):
        rank = last[0, n]

        @pl.when(rank < EARLY)
        def _():
            fetch(n, rank).wait()
            put(n, stage.at[n]).start()

    @pl.loop(0, count, unroll=8)
    def _(n):
        put(n, stage.at[n]).wait()


def on_device(a_panels, b_panels, a_rows, a_inner, b_inner, b_cols, c_rows, c_cols):
    partial, recent, last = gather(a_panels, b_panels, (a_rows, a_inner, b_inner, b_cols, c_rows, c_cols))
    slots, width = c_rows.shape[2], a_panels.shape[3]
    anywhere = pl.BlockSpec(memory_space=pl.ANY)
    return pl.pallas_call(
        place_kernel,
        out_shape=jax.ShapeDtypeStruct((1, 1, slots, width, width), a_panels.dtype),
        grid_spec=pltpu.PrefetchScalarGridSpec(
            num_scalar_prefetch=1,
            grid=(),
            in_specs=[pl.BlockSpec(memory_space=pltpu.HBM), anywhere],
            out_specs=anywhere,
            scratch_shapes=[
                pltpu.VMEM((slots, width, width), a_panels.dtype),
                pltpu.SemaphoreType.DMA((slots,)),
                pltpu.SemaphoreType.DMA((slots,)),
            ],
        ),
        compiler_params=pltpu.CompilerParams(vmem_limit_bytes=38000000),
        name="place",
    )(last, partial, recent)


def solution(mesh):
    in_specs = (
        P("row", "col", None, None, None),
        P("row", "col", None, None, None),
        P(),
        P(),
        P(),
        P(),
        P(),
        P(),
    )
    out_specs = P("row", "col", None, None, None)
    return jax.shard_map(
        on_device, mesh=mesh, in_specs=in_specs, out_specs=out_specs, check_vma=False
    )
```
